128 devices in a mesh: lat: 8 (over z, core), lon: 16 (over x, y).
Axes of the slice: x: 4, y: 4, z: 4, core: 2. Of those that a mesh axis runs over, the one named last changes fastest.
Arguments:
- sensitivity: bfloat16 [8, 16, 60, 256, 128], P('lat', 'lon'), may hold values from 0 to 0.07470703
- block_ids: int32 [8, 16, 60], P('lat', 'lon'), may hold values from 0 to 131071, as said below
- block_offsets: int32 [8, 16, 4], P('lat', 'lon'), may hold values from 0 to 60, as said below
- ray_counts: int32 [8, 16], P('lat', 'lon'), may hold values from 1 to 768, as said below
- ray_vector: float32 [4, 8, 16, 768], P(None, 'lat', 'lon'), may hold values from -6 to 6
- damping_vector: float32 [4, 256, 512, 128], P(None, 'lat', 'lon'), may hold values from -6 to 6
- model_vector: float32 [4, 256, 512, 128], P(None, 'lat', 'lon'), may hold values from -6 to 6
- solution: float32 [4, 256, 512, 128], P(None, 'lat', 'lon'), may hold values from -6 to 6
- search: float32 [4, 256, 512, 128], P(None, 'lat', 'lon'), may hold values from -6 to 6
- recurrence: float32 [3, 4], replicated, may hold values from 0.5 to 1.5
Outputs:
- ray_out: float32 [4, 8, 16, 768], P(None, 'lat', 'lon')
- damp_out: float32 [4, 256, 512, 128], P(None, 'lat', 'lon')
- model_out: float32 [4, 256, 512, 128], P(None, 'lat', 'lon')
- solution_out: float32 [4, 256, 512, 128], P(None, 'lat', 'lon')
- search_out: float32 [4, 256, 512, 128], P(None, 'lat', 'lon')
- recurrence_out: float32 [3, 4], replicated
The draws below stay inside these ranges and needn't reach their ends.
Inputs may be any that keep to these rules, and one draw needn't show every extreme that they name: `block_ids`: of the 60 entries of one device at most 2 name blocks of one owner device; some owner is named exactly 2 times by every device. Entries of tiles that belong to no ray block name blocks too. The entries of all devices that name one owner's blocks lie in one patch of 4 x 4 neighbouring columns of that owner. `block_offsets`: each device's offsets start at 0 and never fall; a ray block holding some live ray has 10 to 20 tiles, the others none; some device uses all 60 tiles. A device's live rays are its first ray_counts rays; some device has all 768 live.
All inputs are finite; a program needn't handle non-finite values.
Results may differ from the reference program's by a relative error of at most 0.0003.
Values may be sent and summed in bfloat16 or wider, within the bound.
A program may use at most 64 MiB of HBM per device.

```python
import jax
import jax.numpy as jnp
from jax import lax

DEPTH = 128
RAYS_BLK = 256
R = 4
KPB = 20
CLAT = 32
CLON = 32
RBMAX = 3
TILES = 60
RAYS = 768
BLK = 1024
CAP = 2
NLAT = 256
NLON = 512
CELLS = 16777216
ROWS_ALL = 16875520
N_LAT = 8
N_LON = 16


def layout(key):
    devices = N_LAT * N_LON
    span = RBMAX * RAYS_BLK
    slots = devices * CAP
    keys = jax.random.split(jax.random.fold_in(key, 7321), 10)
    place = jnp.arange(devices, dtype=jnp.int32)
    raw = jax.random.randint(keys[0], (devices,), 0, span, dtype=jnp.int32)
    counts = 1 + raw * raw // span
    fullest = jax.random.randint(keys[1], (), 0, devices, dtype=jnp.int32)
    counts = jnp.where(place == fullest, span, counts).astype(jnp.int32)
    live_blocks = (counts + RAYS_BLK - 1) // RAYS_BLK
    per_block = jax.random.randint(keys[2], (devices, RBMAX), KPB // 2, KPB + 1, dtype=jnp.int32)
    per_block = jnp.where(place[:, None] == fullest, KPB, per_block)
    per_block = jnp.where(jnp.arange(RBMAX, dtype=jnp.int32)[None, :] < live_blocks[:, None], per_block, 0)
    offsets = jnp.concatenate([jnp.zeros((devices, 1), jnp.int32), jnp.cumsum(per_block, axis=1).astype(jnp.int32)], axis=1)
    hottest = jax.random.randint(keys[3], (), 0, devices, dtype=jnp.int32)
    orders = jax.vmap(lambda sub: jax.random.permutation(sub, slots))(jax.random.split(keys[4], devices)).astype(jnp.int32)
    priority = jnp.where(orders // CAP == hottest, 0, slots) + jnp.arange(slots, dtype=jnp.int32)[None, :]
    ranking = jnp.argsort(priority, axis=1)
    chosen = jnp.take_along_axis(orders, ranking[:, :TILES], axis=1)
    shuffle = jax.vmap(lambda sub: jax.random.permutation(sub, TILES))(jax.random.split(keys[5], devices))
    chosen = jnp.take_along_axis(chosen, shuffle, axis=1)
    owner = (chosen // CAP).astype(jnp.int32)
    corner_lat = jax.random.randint(keys[7], (devices,), 0, CLAT - 3, dtype=jnp.int32)
    corner_lon = jax.random.randint(keys[8], (devices,), 0, CLON - 3, dtype=jnp.int32)
    step_lat = jax.random.randint(keys[6], (devices, TILES), 0, 4, dtype=jnp.int32)
    step_lon = jax.random.randint(keys[9], (devices, TILES), 0, 4, dtype=jnp.int32)
    column = (corner_lat[owner] + step_lat) * CLON + corner_lon[owner] + step_lon
    block_list = (owner * BLK + column).astype(jnp.int32)
    return (counts, offsets, block_list)


def draw_block_ids(key, part):
    return layout(key)[2].reshape(N_LAT, N_LON, TILES)


def draw_block_offsets(key, part):
    return layout(key)[1].reshape(N_LAT, N_LON, RBMAX + 1)


def draw_ray_counts(key, part):
    return layout(key)[0].reshape(N_LAT, N_LON)


def draw_model_vector(key, part):
    level_key, noise_key = jax.random.split(jax.random.fold_in(key, 4409))
    level = jax.random.uniform(level_key, (R, NLAT, NLON, 1), jnp.float32, 0.5, 1.5)
    noise = jnp.clip(jax.random.normal(noise_key, (R, NLAT, NLON, DEPTH), jnp.float32), -4.0, 4.0)
    return (level + noise).astype(jnp.float32)


def block_levels(own_key, shape, shards, least, high):
    gain, own = 1.0, jax.random.fold_in(own_key, 6)
    for axis_at, parts in shards:
        steps = jnp.exp(jax.random.uniform(jax.random.fold_in(own, axis_at), (parts,), jnp.float32, least / len(shards), high / len(shards)))
        gain = gain * jnp.repeat(steps, shape[axis_at] // parts).reshape([-1 if axis == axis_at else 1 for axis in range(len(shape))])
    return gain


def bell_draw(key, extent, scale, limit, cuts=(), kind=jnp.bfloat16):
    factor_of = block_levels(key, extent, cuts, -0.22, 0.18) if cuts else 1.0
    result = jax.random.normal(key, extent, jnp.float32) * scale * factor_of
    return jnp.minimum(jnp.maximum(result, -limit), limit).astype(kind)


def setup_inputs(seed: int = 0) -> dict:
    arg_keys = jax.random.split(jax.random.key(seed), 11)
    sensitivity = jnp.clip(0.07470703 * jax.random.uniform(arg_keys[0], (N_LAT, N_LON, TILES, RAYS_BLK, DEPTH), jnp.float32) ** block_levels(arg_keys[0], (N_LAT, N_LON, TILES, RAYS_BLK, DEPTH), ((0, 8), (1, 16)), -0.2, 0.2), 0.0, 0.07470703).astype(jnp.bfloat16)
    block_ids = draw_block_ids(jax.random.fold_in(arg_keys[10], 71), 0)
    block_offsets = draw_block_offsets(jax.random.fold_in(arg_keys[10], 71), 0)
    ray_counts = draw_ray_counts(jax.random.fold_in(arg_keys[10], 71), 0)
    ray_vector = bell_draw(arg_keys[4], (R, N_LAT, N_LON, RAYS), 1.0, 6.0, ((1, 8), (2, 16)), jnp.float32)
    damping_vector = bell_draw(arg_keys[5], (R, NLAT, NLON, DEPTH), 1.0, 6.0, ((1, 8), (2, 16)), jnp.float32)
    model_vector = draw_model_vector(jax.random.fold_in(arg_keys[10], 71), 0)
    solution = bell_draw(arg_keys[7], (R, NLAT, NLON, DEPTH), 1.0, 6.0, ((1, 8), (2, 16)), jnp.float32)
    search = bell_draw(arg_keys[8], (R, NLAT, NLON, DEPTH), 1.0, 6.0, ((1, 8), (2, 16)), jnp.float32)
    recurrence = jnp.clip(jax.random.uniform(arg_keys[9], (3, R), jnp.float32, 0.5, 1.5), 0.5, 1.5)
    return dict(sensitivity=sensitivity, block_ids=block_ids, block_offsets=block_offsets, ray_counts=ray_counts, ray_vector=ray_vector, damping_vector=damping_vector, model_vector=model_vector, solution=solution, search=search, recurrence=recurrence)


DAMP_WEIGHT = 0.15
EPSILON = 1e-05
HIGHEST_PRECISION = lax.Precision.HIGHEST

def laplace(field):
    padded = jnp.pad(field, ((0, 0), (1, 1), (1, 1), (1, 1)))
    beside_all = padded[:, 2:, 1:-1, 1:-1] + padded[:, :-2, 1:-1, 1:-1]
    beside_all = beside_all + padded[:, 1:-1, 2:, 1:-1] + padded[:, 1:-1, :-2, 1:-1]
    beside_all = beside_all + padded[:, 1:-1, 1:-1, 2:] + padded[:, 1:-1, 1:-1, :-2]
    return 6.0 * field - beside_all

def to_table(field):
    shaped = field.reshape(R, N_LAT, CLAT, N_LON, CLON, DEPTH)
    return shaped.transpose(1, 3, 2, 4, 0, 5).reshape(N_LAT * N_LON * CLAT * CLON, R, DEPTH)

def from_table(table):
    shaped = table.reshape(N_LAT, N_LON, CLAT, CLON, R, DEPTH)
    return shaped.transpose(4, 0, 2, 1, 3, 5).reshape(R, N_LAT * CLAT, N_LON * CLON, DEPTH)

def membership(limits):
    position = jnp.arange(TILES, dtype=jnp.int32)[:, None]
    inside = (position >= limits[None, :-1]) & (position < limits[None, 1:])
    return inside.astype(jnp.float32)

def reference(sensitivity, block_ids, block_offsets, ray_counts, ray_vector, damping_vector, model_vector, solution, search, recurrence):
    devices = N_LAT * N_LON
    alpha_old = recurrence[0]
    rho_bar = recurrence[1]
    phi_bar = recurrence[2]
    kernels = sensitivity.reshape(devices, TILES, RAYS_BLK, DEPTH)
    block_list = block_ids.reshape(devices, TILES)
    bounds = block_offsets.reshape(devices, RBMAX + 1)
    counts = ray_counts.reshape(devices)
    ray_old = ray_vector.reshape(R, devices, RBMAX, RAYS_BLK)
    model_low = to_table(model_vector).astype(jnp.bfloat16)

    def forward(operands):
        kernel, listed, limits = operands
        picked = model_low[listed].astype(jnp.float32)
        products = jnp.einsum('tid,trd->tri', kernel.astype(jnp.float32), picked, precision=HIGHEST_PRECISION)
        return jnp.einsum('tb,tri->rbi', membership(limits), products, precision=HIGHEST_PRECISION)
    traced = lax.map(forward, (kernels, block_list, bounds)).transpose(1, 0, 2, 3)
    ray_index = jnp.arange(RBMAX * RAYS_BLK, dtype=jnp.int32).reshape(RBMAX, RAYS_BLK)
    live_rows = ray_index[None, :, :] < counts[:, None, None]
    alpha_wide = alpha_old[:, None, None, None]
    ray_bar = jnp.where(live_rows[None], traced - alpha_wide * ray_old, 0.0)
    damp_bar = DAMP_WEIGHT * laplace(model_vector) - alpha_wide * damping_vector
    residual_sq = lax.optimization_barrier(jnp.sum(ray_bar * ray_bar, axis=(1, 2, 3))) + lax.optimization_barrier(jnp.sum(damp_bar * damp_bar, axis=(1, 2, 3)))
    beta_new = jnp.sqrt(residual_sq / ROWS_ALL + EPSILON)
    ray_low = ray_bar.astype(jnp.bfloat16)

    def adjoint(operands):
        kernel, limits, ray_rows = operands
        spread = jnp.einsum('tb,rbi->tri', membership(limits), ray_rows.astype(jnp.float32), precision=HIGHEST_PRECISION)
        return jnp.einsum('tid,tri->trd', kernel.astype(jnp.float32), spread, precision=HIGHEST_PRECISION)
    pieces = lax.map(adjoint, (kernels, bounds, ray_low.transpose(1, 0, 2, 3)))
    summed = jax.ops.segment_sum(pieces.reshape(devices * TILES, R, DEPTH), block_list.reshape(devices * TILES), num_segments=devices * CLAT * CLON)
    adjoint_image = from_table(summed) + DAMP_WEIGHT * laplace(damp_bar)
    beta_wide = beta_new[:, None, None, None]
    update = adjoint_image / beta_wide - beta_wide * model_vector
    alpha_new = jnp.sqrt(lax.optimization_barrier(jnp.sum(update * update, axis=(1, 2, 3))) / CELLS + EPSILON)
    model_out = update / alpha_new[:, None, None, None]
    rho_new = jnp.sqrt(rho_bar * rho_bar + beta_new * beta_new)
    cosine = rho_bar / rho_new
    sine_new = beta_new / rho_new
    solution_out = solution + (cosine * phi_bar / rho_new)[:, None, None, None] * search
    search_out = model_out - (sine_new * alpha_new / rho_new)[:, None, None, None] * search
    ray_out = (ray_bar / beta_wide).reshape(R, N_LAT, N_LON, RBMAX * RAYS_BLK)
    damp_out = damp_bar / beta_wide
    recurrence_out = jnp.stack([alpha_new, -cosine * alpha_new, sine_new * phi_bar])
    return (ray_out, damp_out, model_out, solution_out, search_out, recurrence_out)
```

```python
import jax
import jax.numpy as jnp
from jax import lax
from jax.experimental import pallas as pl
from jax.experimental.pallas import tpu as pltpu
from jax.sharding import PartitionSpec as P

DAMP_WEIGHT = 0.15
EPSILON = 1e-05
HIGHEST_PRECISION = lax.Precision.HIGHEST


MESH = pl.DeviceIdType.MESH


def share_kernel(value_ref, all_ref, send_sem, recv_sem):
    lat_size = lax.axis_size("lat")
    lon_size = lax.axis_size("lon")
    devices = lat_size * lon_size
    me = lax.axis_index("lat") * lon_size + lax.axis_index("lon")
    barrier = pltpu.get_barrier_semaphore()

    def greet(step, carry):
        other = lax.rem(me + step, devices)
        place = (other // lon_size, lax.rem(other, lon_size))
        pl.semaphore_signal(barrier, inc=1, device_id=place, device_id_type=MESH)
        return carry

    lax.fori_loop(1, devices, greet, 0)
    all_ref[me] = value_ref[...]
    pl.semaphore_wait(barrier, devices - 1)

    def send(step, carry):
        other = lax.rem(me + step, devices)
        place = (other // lon_size, lax.rem(other, lon_size))
        pltpu.make_async_remote_copy(
            value_ref, all_ref.at[me], send_sem, recv_sem, device_id=place, device_id_type=MESH
        ).start()
        return carry

    lax.fori_loop(1, devices, send, 0)
    most = all_ref.at[pl.ds(0, devices - 1)]
    pltpu.make_async_copy(most, most, recv_sem).wait()
    pltpu.make_async_copy(most, most, send_sem).wait()


def total(value):
    devices = lax.axis_size("lat") * lax.axis_size("lon")
    wide = jnp.pad(value[None], ((0, 0), (0, 128 - value.shape[0])))
    gathered = pl.pallas_call(
        share_kernel,
        out_shape=jax.ShapeDtypeStruct((devices, 1, 128), jnp.float32),
        in_specs=[pl.BlockSpec(memory_space=pltpu.VMEM)],
        out_specs=pl.BlockSpec(memory_space=pltpu.VMEM),
        scratch_shapes=[pltpu.SemaphoreType.DMA, pltpu.SemaphoreType.DMA],
        compiler_params=pltpu.CompilerParams(collective_id=0, has_side_effects=True),
        name="share",
    )(wide)
    return jnp.sum(gathered[:, 0, : value.shape[0]], axis=0)


def with_halo(cells, sides, width):
    for axis, dim in sides:
        count = lax.axis_size(axis)
        ends = count - 1
        head = lax.slice_in_dim(cells, 0, width, axis=dim)
        tail = lax.slice_in_dim(cells, cells.shape[dim] - width, cells.shape[dim], axis=dim)
        cells = jnp.concatenate(
            [
                lax.ppermute(tail, axis, [(i, (i + 1) % count) for i in range(ends)]),
                cells,
                lax.ppermute(head, axis, [((i + 1) % count, i) for i in range(ends)]),
            ],
            axis=dim,
        )
    return cells


def laplace(field):
    padded = with_halo(field, (("lat", 1), ("lon", 2)), 1)
    depth_pad = jnp.pad(field, ((0, 0), (0, 0), (0, 0), (1, 1)))
    beside_all = (
        padded[:, 2:, 1:-1] + padded[:, :-2, 1:-1] + padded[:, 1:-1, 2:] + padded[:, 1:-1, :-2]
    )
    beside_all = beside_all + depth_pad[..., 2:] + depth_pad[..., :-2]
    return 6.0 * field - beside_all


def membership(limits, tiles):
    position = jnp.arange(tiles, dtype=jnp.int32)[:, None]
    inside = (position >= limits[None, :-1]) & (position < limits[None, 1:])
    return inside.astype(jnp.float32)


def per_device(
    sensitivity,
    block_ids,
    block_offsets,
    ray_counts,
    ray_vector,
    damping_vector,
    model_vector,
    solution,
    search,
    recurrence,
):
    lat_size = lax.axis_size("lat")
    lon_size = lax.axis_size("lon")
    devices = lat_size * lon_size
    kernel = sensitivity[0, 0]
    tiles, ray_width, depth = kernel.shape
    block_list = block_ids[0, 0]
    bounds = block_offsets[0, 0]
    count_here = ray_counts[0, 0]
    blocks_dev = bounds.shape[0] - 1
    systems, clat_dev, clon_dev = (
        model_vector.shape[0],
        model_vector.shape[1],
        model_vector.shape[2],
    )
    columns_dev = clat_dev * clon_dev
    capacity = 2 * ((tiles + devices - 1) // devices)
    cells_all = devices * columns_dev * depth
    rows_all = devices * blocks_dev * ray_width + cells_all
    alpha_old = recurrence[0]
    rho_bar = recurrence[1]
    phi_bar = recurrence[2]
    owner_dev = block_list // columns_dev
    column = block_list - owner_dev * columns_dev
    owner_hits = (owner_dev[:, None] == jnp.arange(devices, dtype=jnp.int32)[None, :]).astype(
        jnp.int32
    )
    slot_rank = jnp.sum(owner_hits * (jnp.cumsum(owner_hits, axis=0) - 1), axis=1)
    slot_index = owner_dev * capacity + slot_rank
    request = jnp.zeros((devices * capacity,), jnp.int32).at[slot_index].set(column + 1)
    wanted = lax.all_to_all(request, ("lat", "lon"), split_axis=0, concat_axis=0, tiled=True)
    table = (
        model_vector.transpose(1, 2, 0, 3).reshape(columns_dev, systems, depth).astype(jnp.bfloat16)
    )
    served = jnp.where(
        (wanted > 0)[:, None, None],
        jnp.take(table, jnp.maximum(wanted - 1, 0), axis=0),
        jnp.zeros((), jnp.bfloat16),
    )
    fetched = lax.all_to_all(served, ("lat", "lon"), split_axis=0, concat_axis=0, tiled=True)
    tile_model = jnp.take(fetched, slot_index, axis=0)
    member = membership(bounds, tiles)
    products = jnp.einsum("tid,trd->tri", kernel, tile_model, preferred_element_type=jnp.float32)
    traced = jnp.einsum("tb,tri->rbi", member, products, precision=HIGHEST_PRECISION)
    ray_old = ray_vector.reshape(systems, blocks_dev, ray_width)
    ray_index = jnp.arange(blocks_dev * ray_width, dtype=jnp.int32).reshape(blocks_dev, ray_width)
    live_rows = ray_index < count_here
    ray_bar = jnp.where(live_rows[None], traced - alpha_old[:, None, None] * ray_old, 0.0)
    damp_bar = DAMP_WEIGHT * laplace(model_vector) - alpha_old[:, None, None, None] * damping_vector
    residual_sq = jnp.sum(ray_bar * ray_bar, axis=(1, 2)) + jnp.sum(
        damp_bar * damp_bar, axis=(1, 2, 3)
    )
    ray_low = ray_bar.astype(jnp.bfloat16)
    spread = jnp.einsum(
        "tb,rbi->tri", member.astype(jnp.bfloat16), ray_low, preferred_element_type=jnp.float32
    ).astype(jnp.bfloat16)
    sent_terms = jnp.einsum("tid,tri->trd", kernel, spread, preferred_element_type=jnp.float32)
    outgoing = (
        jnp.zeros((devices * capacity, systems, depth), jnp.float32).at[slot_index].set(sent_terms)
    )
    incoming = lax.all_to_all(outgoing, ("lat", "lon"), split_axis=0, concat_axis=0, tiled=True)
    collected = jnp.zeros((columns_dev + 1, systems, depth), jnp.float32).at[wanted].add(incoming)
    remote_part = collected[1:].reshape(clat_dev, clon_dev, systems, depth).transpose(2, 0, 1, 3)
    adjoint_image = remote_part + DAMP_WEIGHT * laplace(damp_bar)
    residual_sq = total(residual_sq)
    beta_new = jnp.sqrt(residual_sq / rows_all + EPSILON)
    beta_wide = beta_new[:, None, None, None]
    update = adjoint_image / beta_wide - beta_wide * model_vector
    update_sq = total(jnp.sum(update * update, axis=(1, 2, 3)))
    alpha_new = jnp.sqrt(update_sq / cells_all + EPSILON)
    model_out = update / alpha_new[:, None, None, None]
    rho_new = jnp.sqrt(rho_bar * rho_bar + beta_new * beta_new)
    cosine = rho_bar / rho_new
    sine_new = beta_new / rho_new
    solution_out = solution + (cosine * phi_bar / rho_new)[:, None, None, None] * search
    search_out = model_out - (sine_new * alpha_new / rho_new)[:, None, None, None] * search
    ray_out = (ray_bar / beta_new[:, None, None]).reshape(systems, 1, 1, blocks_dev * ray_width)
    damp_out = damp_bar / beta_wide
    recurrence_out = jnp.stack([alpha_new, -cosine * alpha_new, sine_new * phi_bar])
    return (ray_out, damp_out, model_out, solution_out, search_out, recurrence_out)


def solution(mesh):
    return jax.shard_map(
        per_device,
        mesh=mesh,
        in_specs=(
            P("lat", "lon", None, None, None),
            P("lat", "lon", None),
            P("lat", "lon", None),
            P("lat", "lon"),
            P(None, "lat", "lon", None),
            P(None, "lat", "lon", None),
            P(None, "lat", "lon", None),
            P(None, "lat", "lon", None),
            P(None, "lat", "lon", None),
            P(),
        ),
        out_specs=(
            P(None, "lat", "lon", None),
            P(None, "lat", "lon", None),
            P(None, "lat", "lon", None),
            P(None, "lat", "lon", None),
            P(None, "lat", "lon", None),
            P(),
        ),
        check_vma=False,
    )
```

```python
import jax
import jax.numpy as jnp
from jax import lax
from jax.experimental import pallas as pl
from jax.experimental.pallas import tpu as pltpu
from jax.sharding import PartitionSpec as P

DAMP_WEIGHT = 0.15
EPSILON = 1e-05
MESH = pl.DeviceIdType.MESH
F32 = jnp.float32
BF16 = jnp.bfloat16

R = 4
CLAT = 32
CLON = 32
DEPTH = 128
BLK = CLAT * CLON
TILES = 60
RAYS_BLK = 256
RBMAX = 3
N_LAT = 8
N_LON = 16
NDEV = N_LAT * N_LON
LAT_PAD = CLAT + 2
LON_PAD = CLON + 16
LEFT = 8
ROWS_ALL = NDEV * RBMAX * RAYS_BLK + NDEV * BLK * DEPTH
CELLS = NDEV * BLK * DEPTH
INNER = pl.ds(LEFT, CLON)


def iota(shape, axis):
    return lax.broadcasted_iota(jnp.int32, shape, axis)


def one(cond):
    return jnp.where(cond, 1.0, 0.0)


def dot(a, b):
    return jnp.dot(a, b, preferred_element_type=F32)


def laplace_slab(ref, r, row):
    here = ref[r, row + 1, INNER]
    beside = ref[r, row, INNER] + ref[r, row + 2, INNER]
    beside = beside + ref[r, row + 1, pl.ds(LEFT - 1, CLON)] + ref[r, row + 1, pl.ds(LEFT + 1, CLON)]
    lane = iota((CLON, DEPTH), 1)
    above = jnp.where(lane == 0, 0.0, pltpu.roll(here, 1, 1))
    below = jnp.where(lane == DEPTH - 1, 0.0, pltpu.roll(here, DEPTH - 1, 1))
    return 6.0 * here - (beside + above + below)


def fold(x):
    return x[0:8] + x[8:16] + x[16:24] + x[24:32]


def step_kernel(
    ids_s, off_s, cnt_s, rec_s, ids_v, rec_v, ray_v, sens_h, damp_h, model_h, sol_h, search_h,
    upd_o, damp_o, sol_o, search_o, coef_o, ray_o, rec_o,
    mp, dp, dv, sens, idrow, ids_all, idcol, slotcol, rowval, sel, selt, oh, oht,
    resp, fetched, wts, terms, outg, inc, zbuf, sum_a, sums_a, sum_b, sums_b,
    edge_s, edge_r, row_r, ray_keep,
    load_sem, send_sem, recv_sem, edge_ssem, edge_rsem,
):
    my_lat = lax.axis_index("lat")
    my_lon = lax.axis_index("lon")
    me = my_lat * N_LON + my_lon

    def place(other):
        return (other // N_LON, lax.rem(other, N_LON))

    barrier = pltpu.get_barrier_semaphore()

    def greet(step, carry):
        other = lax.rem(me + step, NDEV)
        pl.semaphore_signal(barrier, inc=1, device_id=place(other), device_id_type=MESH)
        return carry

    lax.fori_loop(1, NDEV, greet, 0)

    loads = [
        pltpu.make_async_copy(model_h, mp.at[:, pl.ds(1, CLAT), INNER, :], load_sem.at[0]),
        pltpu.make_async_copy(damp_h, dv, load_sem.at[1]),
        pltpu.make_async_copy(sens_h, sens, load_sem.at[2]),
        pltpu.make_async_copy(sol_h, sol_o, load_sem.at[3]),
        pltpu.make_async_copy(search_h, search_o, load_sem.at[4]),
    ]
    for load in loads:
        load.start()

    idrow[...] = jnp.full((1, 128), -1, jnp.int32)
    idrow[:, 0:TILES] = ids_v[...]

    side = jnp.zeros((R, LAT_PAD, LEFT, DEPTH), F32)
    mp[:, :, pl.ds(0, LEFT), :] = side
    mp[:, :, pl.ds(LEFT + CLON, LEFT), :] = side
    dp[:, :, pl.ds(0, LEFT), :] = side
    dp[:, :, pl.ds(LEFT + CLON, LEFT), :] = side
    flat = jnp.zeros((R, CLON, DEPTH), F32)

    @pl.when(my_lat == 0)
    def _():
        mp[:, 0, INNER, :] = flat
        dp[:, 0, INNER, :] = flat

    @pl.when(my_lat == N_LAT - 1)
    def _():
        mp[:, LAT_PAD - 1, INNER, :] = flat
        dp[:, LAT_PAD - 1, INNER, :] = flat

    for t in range(TILES):
        idcol[t : t + 1, :] = jnp.full((1, 128), ids_s[0, t], jnp.int32)
    idcol[TILES:64, :] = jnp.full((64 - TILES, 128), -1, jnp.int32)
    owner_col = idcol[...] >> 10
    owner_row = jnp.broadcast_to(idrow[...] >> 10, (64, 128))
    twin = one((owner_col == owner_row) & (iota((64, 128), 1) < iota((64, 128), 0)))
    rank = jnp.max(twin, axis=1, keepdims=True).astype(jnp.int32)
    slotcol[...] = jnp.where(iota((64, 128), 0) < TILES, (owner_col * 2 + rank) * 4, -64)

    row16 = iota((16, 128), 0)
    blk16 = row16 // 4
    first16 = jnp.where(blk16 == 0, off_s[0, 0], jnp.where(blk16 == 1, off_s[0, 1], off_s[0, 2]))
    last16 = jnp.where(
        blk16 == 0, off_s[0, 1],
        jnp.where(blk16 == 1, off_s[0, 2], jnp.where(blk16 == 2, off_s[0, 3], 0)),
    )
    lane16 = iota((16, 128), 1)

    def build_sel(t, carry):
        slot = jnp.broadcast_to(slotcol[pl.ds(t, 1), :], (16, 128))
        value = jnp.where((first16 <= t) & (t < last16), slot + (row16 & 3), -1)
        rows = pl.ds(pl.multiple_of(t * 16, 16), 16)
        rowval[rows, :] = value.astype(F32)
        for j in range(8):
            sel[rows, j * 128 : (j + 1) * 128] = one(value == lane16 + j * 128).astype(BF16)
        return carry

    lax.fori_loop(0, 64, build_sel, 0, unroll=2)

    pl.semaphore_wait(barrier, NDEV - 1)

    def share(src, dst, k):
        def send(step, carry):
            other = lax.rem(me + step, NDEV)
            pltpu.make_async_remote_copy(
                src, dst.at[me], send_sem.at[k], recv_sem.at[k],
                device_id=place(other), device_id_type=MESH,
            ).start()
            return carry

        lax.fori_loop(1, NDEV, send, 0)
        dst[me] = src[...]

    def settle(dst, sem):
        most = dst.at[pl.ds(0, NDEV - 1)]
        pltpu.make_async_copy(most, most, sem).wait()

    share(idrow, ids_all, 0)

    def edge(buf, k, base):
        n = base + k
        if k == 0:
            src, dst, to = buf.at[:, 1, INNER, :], row_r.at[base // 4, 1], (my_lat - 1, my_lon)
        elif k == 1:
            src, dst, to = buf.at[:, CLAT, INNER, :], row_r.at[base // 4, 0], (my_lat + 1, my_lon)
        elif k == 2:
            src, dst, to = edge_s.at[base // 4, 0], edge_r.at[base // 4, 1], (my_lat, my_lon - 1)
        else:
            src, dst, to = edge_s.at[base // 4, 1], edge_r.at[base // 4, 0], (my_lat, my_lon + 1)
        return pltpu.make_async_remote_copy(
            src, dst, edge_ssem.at[n], edge_rsem.at[n], device_id=to, device_id_type=MESH
        )

    has = [my_lat > 0, my_lat < N_LAT - 1, my_lon > 0, my_lon < N_LON - 1]
    opposite = [1, 0, 3, 2]

    def send_edges(buf, base):
        for r in range(R):
            edge_s[base // 4, 0, r] = buf[r, pl.ds(1, CLAT), LEFT, :]
            edge_s[base // 4, 1, r] = buf[r, pl.ds(1, CLAT), LEFT + CLON - 1, :]
        for k in range(4):
            @pl.when(has[k])
            def _(k=k):
                edge(buf, k, base).start()

    def take_edges(buf, base):
        for k in range(4):
            @pl.when(has[k])
            def _(k=k):
                edge(buf, opposite[k], base).wait_recv()
                edge(buf, k, base).wait_send()
        for k, row in ((0, 0), (1, LAT_PAD - 1)):
            @pl.when(has[k])
            def _(k=k, row=row):
                for r in range(R):
                    buf[r, row, INNER, :] = row_r[base // 4, k, r]
        for k, column in ((2, LEFT - 1), (3, LEFT + CLON)):
            @pl.when(has[k])
            def _(k=k, column=column):
                for r in range(R):
                    buf[r, pl.ds(1, CLAT), column, :] = edge_r[base // 4, k - 2, r]

    loads[0].wait()
    send_edges(mp, 0)

    def build_selt(g, carry):
        rows = pl.ds(pl.multiple_of(g * 16, 16), 16)
        number = (row16 + g * 16).astype(F32)
        for j in range(8):
            lanes = jnp.broadcast_to(rowcol[j], (16, 128))
            selt[rows, j * 128 : (j + 1) * 128] = one(lanes == number).astype(BF16)
        return carry

    rowcol = [rowval[j * 128 : (j + 1) * 128, :].T[0:1, :] for j in range(8)]
    lax.fori_loop(0, 64, build_selt, 0, unroll=2)
    zbuf[...] = jnp.zeros_like(zbuf)
    terms[TILES * 16 : 1024, :] = jnp.zeros((1024 - TILES * 16, 256), BF16)

    settle(ids_all, recv_sem.at[0])
    asked = ids_all[...]
    mine = (asked >> 10) == me
    lat0 = jnp.min(jnp.where(mine, (asked >> 5) & 31, CLAT - 4))
    lon0 = jnp.min(jnp.where(mine, asked & 31, CLON - 4))
    patch = jnp.concatenate(
        [mp[r, lat0 + i + 1, pl.ds(LEFT + lon0, 8), :] for r in range(R) for i in range(4)], axis=0
    ).astype(BF16)

    sub3 = iota((16, 8, 128), 1)
    lane3 = iota((16, 8, 128), 2)
    sign3 = jnp.where(sub3 < 4, 1.0, -1.0)

    def turn(c):
        return lax.rem(my_lat + c, N_LAT)

    def serve(c, carry):
        group = turn(c)
        near = jnp.broadcast_to(ids_all[pl.ds(group * 16, 16)], (16, 8, 128))
        cell = (((near >> 5) & 31) - lat0) * 8 + ((near & 31) - lon0)
        key = (lane3 * 64 + cell).astype(F32) * sign3
        least = jnp.min(jnp.where((near >> 10) == me, key, 1e6), axis=2, keepdims=True)
        pick = jnp.abs(least).astype(jnp.int32)
        target = jnp.where(pick < 64 * 128, (sub3 & 3) * 32 + (pick & 63), -1)
        hot = one(lane3 == target).reshape(128, 128).astype(BF16)
        rows = pl.ds(pl.multiple_of(group * 128, 128), 128)
        oh[rows, :] = hot
        resp[pl.ds(group * 16, 16)] = dot(hot, patch).reshape(16, 8, 128).astype(BF16)

        def send(s, carry):
            other = group * 16 + lax.rem(my_lon + s, N_LON)

            @pl.when(other != me)
            def _():
                pltpu.make_async_remote_copy(
                    resp.at[other], fetched.at[me], send_sem.at[1], recv_sem.at[1],
                    device_id=place(other), device_id_type=MESH,
                ).start()

            return carry

        lax.fori_loop(0, N_LON, send, 0)
        return carry

    lax.fori_loop(0, N_LAT, serve, 0)
    fetched[me] = resp[me]

    take_edges(mp, 0)
    loads[1].wait()
    sums = []
    for r in range(R):
        alpha = rec_s[0, r]

        def stencil(row, acc, r=r, alpha=alpha):
            damp = DAMP_WEIGHT * laplace_slab(mp, r, row) - alpha * dv[r, row]
            dp[r, row + 1, INNER] = damp
            return acc + fold(damp * damp)

        sums.append(lax.fori_loop(0, CLAT, stencil, jnp.zeros((8, 128), F32), unroll=2))
    send_edges(dp, 4)
    for j in range(8):
        blk = oh[j * 128 : (j + 1) * 128, :].astype(F32)
        oht[:, j * 128 : (j + 1) * 128] = blk.T.astype(BF16)
    ray_old = jnp.concatenate(
        [ray_v[:, b * RAYS_BLK : (b + 1) * RAYS_BLK] for b in range(RBMAX)]
        + [jnp.zeros((R, RAYS_BLK), F32)],
        axis=0,
    )
    wide16 = iota((16, RAYS_BLK), 0)
    r16 = wide16 & 3
    alpha16 = jnp.where(
        r16 == 0, rec_s[0, 0], jnp.where(r16 == 1, rec_s[0, 1], jnp.where(r16 == 2, rec_s[0, 2], rec_s[0, 3]))
    )
    ray_scaled = alpha16 * ray_old
    live = ((wide16 // 4) * RAYS_BLK + iota((16, RAYS_BLK), 1)) < cnt_s[0, 0]
    loads[2].wait()

    settle(fetched, recv_sem.at[1])
    blocks = fetched[...].reshape(1024, 128)
    for j in range(4):
        rows = slice(j * 256, (j + 1) * 256)
        wts[rows, :] = dot(sel[rows, :], blocks).astype(BF16)

    def forward(t, acc):
        rows = pl.ds(pl.multiple_of(t * 16, 16), 16)
        return acc + lax.dot_general(
            wts[rows, :], sens[t], (((1,), (1,)), ((), ())), preferred_element_type=F32
        )

    traced = lax.fori_loop(0, TILES, forward, jnp.zeros((16, RAYS_BLK), F32), unroll=6)
    ray_bar = jnp.where(live, traced - ray_scaled, 0.0)
    ray_keep[...] = ray_bar
    ray_sq = ray_bar * ray_bar
    ray_sq = ray_sq[:, 0:128] + ray_sq[:, 128:256]
    message = jnp.zeros((1, 128), F32)
    for r in range(R):
        part = jnp.where((row16 & 3) == r, ray_sq, 0.0)
        part = part[0:8] + part[8:16] + sums[r]
        message = jnp.where(iota((1, 128), 1) == r, jnp.sum(part, keepdims=True), message)
    sum_a[...] = message
    share(sum_a, sums_a, 2)

    ray_low = ray_bar.astype(BF16)

    def adjoint(t, carry):
        term = dot(ray_low, sens[t])
        high = term.astype(BF16)
        rows = pl.ds(pl.multiple_of(t * 16, 16), 16)
        terms[rows, 0:128] = high
        terms[rows, 128:256] = (term - high.astype(F32)).astype(BF16)
        return carry

    lax.fori_loop(0, TILES, adjoint, 0, unroll=6)

    def give(c, carry):
        group = turn(c)
        rows = pl.ds(pl.multiple_of(group * 128, 128), 128)
        both = dot(selt[rows, :], terms[...])
        outg[pl.ds(group * 16, 16)] = (both[:, 0:128] + both[:, 128:256]).reshape(16, 8, 128)

        def send(s, carry):
            other = group * 16 + lax.rem(my_lon + s, N_LON)

            @pl.when(other != me)
            def _():
                pltpu.make_async_remote_copy(
                    outg.at[other], inc.at[me], send_sem.at[3], recv_sem.at[3],
                    device_id=place(other), device_id_type=MESH,
                ).start()

            return carry

        lax.fori_loop(0, N_LON, send, 0)
        return carry

    lax.fori_loop(0, N_LAT, give, 0)
    inc[me] = outg[me]

    take_edges(dp, 4)
    for r in range(R):

        def stencil2(row, carry, r=r):
            dv[r, row] = DAMP_WEIGHT * laplace_slab(dp, r, row)
            return carry

        lax.fori_loop(0, CLAT, stencil2, 0, unroll=2)

    settle(sums_a, recv_sem.at[2])
    lane_sum = jnp.sum(sums_a[...], axis=0)[:, 0:R]
    beta = jnp.sqrt(lane_sum / ROWS_ALL + EPSILON)
    inv_beta = 1.0 / beta
    rho_bar = rec_v[1:2, :]
    phi_bar = rec_v[2:3, :]
    rho = jnp.sqrt(rho_bar * rho_bar + beta * beta)
    cosine = rho_bar / rho
    sine = beta / rho

    settle(inc, recv_sem.at[3])
    arrived = inc[...].reshape(1024, 128)
    high = arrived.astype(BF16)
    low = (arrived - high.astype(F32)).astype(BF16)
    image = dot(oht[...], high) + dot(oht[...], low)
    for r in range(R):
        for i in range(4):
            zbuf[r, i, pl.ds(32, 8), :] = image[r * 32 + i * 8 : r * 32 + i * 8 + 8]

    message = jnp.zeros((1, 128), F32)
    for r in range(R):
        beta_r = beta[:, r : r + 1]
        inv_r = inv_beta[:, r : r + 1]

        def renew(row, acc, r=r, beta_r=beta_r, inv_r=inv_r):
            off = row - lat0
            pick = jnp.where((off >= 0) & (off < 4), off, 4)
            extra = zbuf[r, pick, pl.ds(32 - lon0, CLON), :]
            upd = (dv[r, row] + extra) * inv_r - beta_r * mp[r, row + 1, INNER]
            upd_o[r, row] = upd
            return acc + fold(upd * upd)

        acc = lax.fori_loop(0, CLAT, renew, jnp.zeros((8, 128), F32), unroll=2)
        message = jnp.where(iota((1, 128), 1) == r, jnp.sum(acc, keepdims=True), message)
    sum_b[...] = message
    share(sum_b, sums_b, 4)

    loads[3].wait()
    loads[4].wait()
    gain = cosine * phi_bar / rho
    for r in range(R):
        inv_r = inv_beta[:, r : r + 1]
        gain_r = gain[:, r : r + 1]

        def scale(row, carry, r=r, inv_r=inv_r, gain_r=gain_r):
            damp_o[r, row] = dp[r, row + 1, INNER] * inv_r
            sol_o[r, row] = sol_o[r, row] + gain_r * search_o[r, row]
            return carry

        lax.fori_loop(0, CLAT, scale, 0, unroll=2)
        for b in range(RBMAX):
            ray_o[r : r + 1, b * RAYS_BLK : (b + 1) * RAYS_BLK] = (
                ray_keep[4 * b + r : 4 * b + r + 1, :] * inv_r
            )

    settle(sums_b, recv_sem.at[4])
    alpha_new = jnp.sqrt(jnp.sum(sums_b[...], axis=0)[:, 0:R] / CELLS + EPSILON)
    inv_alpha = 1.0 / alpha_new
    back = sine * alpha_new / rho
    for r in range(R):
        coef_o[r : r + 1, :] = jnp.broadcast_to(inv_alpha[:, r : r + 1], (1, 128))
        coef_o[4 + r : 5 + r, :] = jnp.broadcast_to(back[:, r : r + 1], (1, 128))
    rec_o[0:1, :] = alpha_new
    rec_o[1:2, :] = -cosine * alpha_new
    rec_o[2:3, :] = sine * phi_bar
    settle(ids_all, send_sem.at[0])
    settle(fetched, send_sem.at[1])
    settle(sums_a, send_sem.at[2])
    settle(inc, send_sem.at[3])
    settle(sums_b, send_sem.at[4])


def finish_kernel(
    upd, damp, sol, search, coef, ray, rec,
    ray_out, damp_out, model_out, sol_out, search_out, rec_out,
    model_s, search_s, sem,
):
    copies = [
        pltpu.make_async_copy(damp, damp_out, sem.at[0]),
        pltpu.make_async_copy(sol, sol_out, sem.at[1]),
        pltpu.make_async_copy(ray, ray_out, sem.at[2]),
        pltpu.make_async_copy(rec, rec_out, sem.at[3]),
    ]
    for copy in copies:
        copy.start()
    for r in range(R):
        inv_r = coef[r : r + 1, :]
        back_r = coef[4 + r : 5 + r, :]

        def write(row, carry, r=r, inv_r=inv_r, back_r=back_r):
            model = upd[r, row] * inv_r
            model_s[r, row] = model
            search_s[r, row] = model - back_r * search[r, row]
            return carry

        lax.fori_loop(0, CLAT, write, 0, unroll=4)
        for src, dst, k in ((model_s, model_out, 4), (search_s, search_out, 8)):
            copy = pltpu.make_async_copy(src.at[r], dst.at[r], sem.at[k + r])
            copy.start()
            copies.append(copy)
    for copy in copies:
        copy.wait()


def per_device(
    sensitivity, block_ids, block_offsets, ray_counts, ray_vector, damping_vector, model_vector,
    solution, search, recurrence,
):
    field = (R, CLAT, CLON, DEPTH)
    vmem = pl.BlockSpec(memory_space=pltpu.VMEM)
    smem = pl.BlockSpec(memory_space=pltpu.SMEM)
    hbm = pl.BlockSpec(memory_space=pl.ANY)
    ids = block_ids.reshape(1, TILES)
    padded = (R, LAT_PAD, LON_PAD, DEPTH)
    middle = [
        pltpu.VMEM(field, F32), pltpu.VMEM(field, F32), pltpu.VMEM(field, F32), pltpu.VMEM(field, F32),
        pltpu.VMEM((8, 128), F32), pltpu.VMEM((R, RBMAX * RAYS_BLK), F32), pltpu.VMEM((3, R), F32),
    ]
    kept = pl.pallas_call(
        step_kernel,
        out_shape=middle,
        in_specs=[smem, smem, smem, smem, vmem, vmem, vmem, hbm, hbm, hbm, hbm, hbm],
        out_specs=[vmem] * 7,
        scratch_shapes=[
            pltpu.VMEM(padded, F32),
            pltpu.VMEM(padded, F32),
            pltpu.VMEM(field, F32),
            pltpu.VMEM((TILES, RAYS_BLK, DEPTH), BF16),
            pltpu.VMEM((1, 128), jnp.int32),
            pltpu.VMEM((NDEV, 1, 128), jnp.int32),
            pltpu.VMEM((64, 128), jnp.int32),
            pltpu.VMEM((64, 128), jnp.int32),
            pltpu.VMEM((1024, 128), F32),
            pltpu.VMEM((1024, 1024), BF16),
            pltpu.VMEM((1024, 1024), BF16),
            pltpu.VMEM((1024, 128), BF16),
            pltpu.VMEM((128, 1024), BF16),
            pltpu.VMEM((NDEV, 8, 128), BF16),
            pltpu.VMEM((NDEV, 8, 128), BF16),
            pltpu.VMEM((1024, 128), BF16),
            pltpu.VMEM((1024, 256), BF16),
            pltpu.VMEM((NDEV, 8, 128), F32),
            pltpu.VMEM((NDEV, 8, 128), F32),
            pltpu.VMEM((R, 5, 72, DEPTH), F32),
            pltpu.VMEM((1, 128), F32),
            pltpu.VMEM((NDEV, 1, 128), F32),
            pltpu.VMEM((1, 128), F32),
            pltpu.VMEM((NDEV, 1, 128), F32),
            pltpu.VMEM((2, 2, R, CLAT, DEPTH), F32),
            pltpu.VMEM((2, 2, R, CLAT, DEPTH), F32),
            pltpu.VMEM((2, 2, R, CLON, DEPTH), F32),
            pltpu.VMEM((16, RAYS_BLK), F32),
            pltpu.SemaphoreType.DMA((5,)),
            pltpu.SemaphoreType.DMA((5,)),
            pltpu.SemaphoreType.DMA((5,)),
            pltpu.SemaphoreType.DMA((8,)),
            pltpu.SemaphoreType.DMA((8,)),
        ],
        compiler_params=pltpu.CompilerParams(
            collective_id=0, has_side_effects=True, vmem_limit_bytes=48 * 1024 * 1024
        ),
        name="step",
    )(
        ids, block_offsets.reshape(1, RBMAX + 1), ray_counts, recurrence, ids, recurrence,
        ray_vector.reshape(R, RBMAX * RAYS_BLK), sensitivity.reshape(TILES, RAYS_BLK, DEPTH),
        damping_vector, model_vector, solution, search,
    )
    shapes = [(R, RBMAX * RAYS_BLK), field, field, field, field, (3, R)]
    ray_out, damp_out, model_out, sol_out, search_out, rec_out = pl.pallas_call(
        finish_kernel,
        out_shape=[jax.ShapeDtypeStruct(s, F32) for s in shapes],
        in_specs=[vmem] * 7,
        out_specs=[hbm] * 6,
        scratch_shapes=[
            pltpu.VMEM(field, F32), pltpu.VMEM(field, F32), pltpu.SemaphoreType.DMA((12,)),
        ],
        compiler_params=pltpu.CompilerParams(vmem_limit_bytes=24 * 1024 * 1024),
        name="finish",
    )(*kept)
    ray_out = ray_out.reshape(R, 1, 1, RBMAX * RAYS_BLK)
    return (ray_out, damp_out, model_out, sol_out, search_out, rec_out)


def solution(mesh):
    wide = P(None, "lat", "lon", None)
    return jax.shard_map(
        per_device,
        mesh=mesh,
        in_specs=(
            P("lat", "lon", None, None, None),
            P("lat", "lon", None),
            P("lat", "lon", None),
            P("lat", "lon"),
            wide,
            wide,
            wide,
            wide,
            wide,
            P(),
        ),
        out_specs=(wide, wide, wide, wide, wide, P()),
        check_vma=False,
    )
```

```python
import jax
import jax.numpy as jnp
from jax import lax
from jax.experimental import pallas as pl
from jax.experimental.pallas import tpu as pltpu
from jax.sharding import PartitionSpec as P

DAMP_WEIGHT = 0.15
EPSILON = 1e-05
MESH = pl.DeviceIdType.MESH
F32 = jnp.float32
BF16 = jnp.bfloat16

R = 4
CLAT = 32
CLON = 32
DEPTH = 128
BLK = CLAT * CLON
TILES = 60
RAYS_BLK = 256
RBMAX = 3
N_LAT = 8
N_LON = 16
NDEV = N_LAT * N_LON
LAT_PAD = CLAT + 2
LON_PAD = CLON + 16
LEFT = 8
ROWS_ALL = NDEV * RBMAX * RAYS_BLK + NDEV * BLK * DEPTH
CELLS = NDEV * BLK * DEPTH
INNER = pl.ds(LEFT, CLON)


def iota(shape, axis):
    return lax.broadcasted_iota(jnp.int32, shape, axis)


def one(cond):
    return jnp.where(cond, 1.0, 0.0)


def dot(a, b):
    return jnp.dot(a, b, preferred_element_type=F32)


def laplace_slab(ref, r, row):
    here = ref[r, row + 1, INNER]
    beside = ref[r, row, INNER] + ref[r, row + 2, INNER]
    beside = beside + ref[r, row + 1, pl.ds(LEFT - 1, CLON)] + ref[r, row + 1, pl.ds(LEFT + 1, CLON)]
    lane = iota((CLON, DEPTH), 1)
    above = jnp.where(lane == 0, 0.0, pltpu.roll(here, 1, 1))
    below = jnp.where(lane == DEPTH - 1, 0.0, pltpu.roll(here, DEPTH - 1, 1))
    return 6.0 * here - (beside + above + below)


def fold(x):
    return x[0:8] + x[8:16] + x[16:24] + x[24:32]


def step_kernel(
    ids_s, off_s, cnt_s, rec_s, ids_v, rec_v, ray_v, sens_h, damp_h, model_h, sol_h, search_h,
    upd_o, damp_o, sol_o, search_o, coef_o, ray_o, rec_o,
    mp, dp, dv, sens, idrow, ids_all, idcol, slotcol, rowval, sel, selt, oh, oht,
    resp, fetched, wts, terms, outg, inc, zbuf, sum_a, part_a, row_a, sums_a, sum_b, part_b, row_b, sums_b,
    edge_s, edge_r, row_r, ray_keep,
    load_sem, send_sem, recv_sem, edge_ssem, edge_rsem,
):
    my_lat = lax.axis_index("lat")
    my_lon = lax.axis_index("lon")
    me = my_lat * N_LON + my_lon

    barrier = pltpu.get_barrier_semaphore()

    def along_lon(step):
        return (my_lat, lax.rem(my_lon + step, N_LON))

    def along_lat(step):
        return (lax.rem(my_lat + step, N_LAT), my_lon)

    def greet_lon(step, carry):
        pl.semaphore_signal(barrier, inc=1, device_id=along_lon(step), device_id_type=MESH)
        return carry

    def greet_lat(step, carry):
        pl.semaphore_signal(barrier, inc=1, device_id=along_lat(step), device_id_type=MESH)
        return carry

    lax.fori_loop(1, N_LON, greet_lon, 0, unroll=True)
    lax.fori_loop(1, N_LAT, greet_lat, 0, unroll=True)

    loads = [
        pltpu.make_async_copy(model_h, mp.at[:, pl.ds(1, CLAT), INNER, :], load_sem.at[0]),
        pltpu.make_async_copy(damp_h, dv, load_sem.at[1]),
        pltpu.make_async_copy(sens_h, sens, load_sem.at[2]),
        pltpu.make_async_copy(sol_h, sol_o, load_sem.at[3]),
        pltpu.make_async_copy(search_h, search_o, load_sem.at[4]),
    ]
    for load in loads:
        load.start()

    idrow[...] = jnp.full((1, 128), -1, jnp.int32)
    idrow[:, 0:TILES] = ids_v[...]

    side = jnp.zeros((R, LAT_PAD, LEFT, DEPTH), F32)
    mp[:, :, pl.ds(0, LEFT), :] = side
    mp[:, :, pl.ds(LEFT + CLON, LEFT), :] = side
    dp[:, :, pl.ds(0, LEFT), :] = side
    dp[:, :, pl.ds(LEFT + CLON, LEFT), :] = side
    flat = jnp.zeros((R, CLON, DEPTH), F32)

    @pl.when(my_lat == 0)
    def _():
        mp[:, 0, INNER, :] = flat
        dp[:, 0, INNER, :] = flat

    @pl.when(my_lat == N_LAT - 1)
    def _():
        mp[:, LAT_PAD - 1, INNER, :] = flat
        dp[:, LAT_PAD - 1, INNER, :] = flat

    for t in range(TILES):
        idcol[t : t + 1, :] = jnp.full((1, 128), ids_s[0, t], jnp.int32)
    idcol[TILES:64, :] = jnp.full((64 - TILES, 128), -1, jnp.int32)
    owner_col = idcol[...] >> 10
    owner_row = jnp.broadcast_to(idrow[...] >> 10, (64, 128))
    twin = one((owner_col == owner_row) & (iota((64, 128), 1) < iota((64, 128), 0)))
    rank = jnp.max(twin, axis=1, keepdims=True).astype(jnp.int32)
    slotcol[...] = jnp.where(iota((64, 128), 0) < TILES, (owner_col * 2 + rank) * 4, -64)

    row16 = iota((16, 128), 0)
    blk16 = row16 // 4
    first16 = jnp.where(blk16 == 0, off_s[0, 0], jnp.where(blk16 == 1, off_s[0, 1], off_s[0, 2]))
    last16 = jnp.where(
        blk16 == 0, off_s[0, 1],
        jnp.where(blk16 == 1, off_s[0, 2], jnp.where(blk16 == 2, off_s[0, 3], 0)),
    )
    lane16 = iota((16, 128), 1)

    def build_sel(t, carry):
        slot = jnp.broadcast_to(slotcol[pl.ds(t, 1), :], (16, 128))
        value = jnp.where((first16 <= t) & (t < last16), slot + (row16 & 3), -1)
        rows = pl.ds(pl.multiple_of(t * 16, 16), 16)
        rowval[rows, :] = value.astype(F32)
        for j in range(8):
            sel[rows, j * 128 : (j + 1) * 128] = one(value == lane16 + j * 128).astype(BF16)
        return carry

    lax.fori_loop(0, 64, build_sel, 0, unroll=2)

    pl.semaphore_wait(barrier, N_LON - 1 + N_LAT - 1)

    def spread(src, dst, k, count, along):
        def send(step, carry):
            pltpu.make_async_remote_copy(
                src, dst, send_sem.at[k], recv_sem.at[k],
                device_id=along(step), device_id_type=MESH,
            ).start()
            return carry

        lax.fori_loop(1, count, send, 0, unroll=True)

    def settle(dst, sem, rows=NDEV - 1):
        most = dst.at[pl.ds(0, rows)]
        pltpu.make_async_copy(most, most, sem).wait()

    spread(idrow, ids_all.at[me], 0, N_LON, along_lon)
    ids_all[me] = idrow[...]

    def edge(buf, k, base):
        n = base + k
        if k == 0:
            src, dst, to = buf.at[:, 1, INNER, :], row_r.at[base // 4, 1], (my_lat - 1, my_lon)
        elif k == 1:
            src, dst, to = buf.at[:, CLAT, INNER, :], row_r.at[base // 4, 0], (my_lat + 1, my_lon)
        elif k == 2:
            src, dst, to = edge_s.at[base // 4, 0], edge_r.at[base // 4, 1], (my_lat, my_lon - 1)
        else:
            src, dst, to = edge_s.at[base // 4, 1], edge_r.at[base // 4, 0], (my_lat, my_lon + 1)
        return pltpu.make_async_remote_copy(
            src, dst, edge_ssem.at[n], edge_rsem.at[n], device_id=to, device_id_type=MESH
        )

    has = [my_lat > 0, my_lat < N_LAT - 1, my_lon > 0, my_lon < N_LON - 1]
    opposite = [1, 0, 3, 2]

    def send_edges(buf, base):
        for r in range(R):
            edge_s[base // 4, 0, r] = buf[r, pl.ds(1, CLAT), LEFT, :]
            edge_s[base // 4, 1, r] = buf[r, pl.ds(1, CLAT), LEFT + CLON - 1, :]
        for k in range(4):
            @pl.when(has[k])
            def _(k=k):
                edge(buf, k, base).start()

    def take_edges(buf, base):
        for k in range(4):
            @pl.when(has[k])
            def _(k=k):
                edge(buf, opposite[k], base).wait_recv()
                edge(buf, k, base).wait_send()
        for k, row in ((0, 0), (1, LAT_PAD - 1)):
            @pl.when(has[k])
            def _(k=k, row=row):
                for r in range(R):
                    buf[r, row, INNER, :] = row_r[base // 4, k, r]
        for k, column in ((2, LEFT - 1), (3, LEFT + CLON)):
            @pl.when(has[k])
            def _(k=k, column=column):
                for r in range(R):
                    buf[r, pl.ds(1, CLAT), column, :] = edge_r[base // 4, k - 2, r]

    row_ids = ids_all.at[pl.ds(my_lat * N_LON, N_LON)]
    settle(ids_all, recv_sem.at[0], N_LON - 1)
    spread(row_ids, row_ids, 5, N_LAT, along_lat)
    loads[0].wait()
    send_edges(mp, 0)

    def build_selt(g, carry):
        rows = pl.ds(pl.multiple_of(g * 16, 16), 16)
        number = (row16 + g * 16).astype(F32)
        for j in range(8):
            lanes = jnp.broadcast_to(rowcol[j], (16, 128))
            selt[rows, j * 128 : (j + 1) * 128] = one(lanes == number).astype(BF16)
        return carry

    rowcol = [rowval[j * 128 : (j + 1) * 128, :].T[0:1, :] for j in range(8)]
    lax.fori_loop(0, 64, build_selt, 0, unroll=2)
    zbuf[...] = jnp.zeros_like(zbuf)
    terms[TILES * 16 : 1024, :] = jnp.zeros((1024 - TILES * 16, 256), BF16)

    def gather_lon(src, parts, k):
        spread(src, parts.at[my_lon], k, N_LON, along_lon)
        parts[my_lon] = src[...]

    def gather_lat(row_sum, parts, totals, k):
        settle(parts, recv_sem.at[k], N_LON - 1)
        row_sum[...] = jnp.sum(parts[...], axis=0)
        spread(row_sum, totals.at[my_lat], k + 4, N_LAT, along_lat)
        totals[my_lat] = row_sum[...]

    settle(ids_all, recv_sem.at[5], NDEV - N_LON)
    asked = ids_all[...]
    mine = (asked >> 10) == me
    lat0 = jnp.min(jnp.where(mine, (asked >> 5) & 31, CLAT - 4))
    lon0 = jnp.min(jnp.where(mine, asked & 31, CLON - 4))
    patch = jnp.concatenate(
        [mp[r, lat0 + i + 1, pl.ds(LEFT + lon0, 8), :] for r in range(R) for i in range(4)], axis=0
    ).astype(BF16)

    sub3 = iota((16, 8, 128), 1)
    lane3 = iota((16, 8, 128), 2)
    sign3 = jnp.where(sub3 < 4, 1.0, -1.0)

    def turn(c):
        return lax.rem(my_lat + c, N_LAT)

    def deal(src, dst, k, group, first):
        def send(s, carry):
            lon = lax.rem(my_lon + s, N_LON)
            pltpu.make_async_remote_copy(
                src.at[group * N_LON + lon], dst.at[me], send_sem.at[k], recv_sem.at[k],
                device_id=(group, lon), device_id_type=MESH,
            ).start()
            return carry

        lax.fori_loop(first, N_LON, send, 0, unroll=True)

    def serve(c, carry, first=0):
        group = turn(c)
        near = jnp.broadcast_to(ids_all[pl.ds(group * 16, 16)], (16, 8, 128))
        cell = (((near >> 5) & 31) - lat0) * 8 + ((near & 31) - lon0)
        key = (lane3 * 64 + cell).astype(F32) * sign3
        least = jnp.min(jnp.where((near >> 10) == me, key, 1e6), axis=2, keepdims=True)
        pick = jnp.abs(least).astype(jnp.int32)
        target = jnp.where(pick < 64 * 128, (sub3 & 3) * 32 + (pick & 63), -1)
        hot = one(lane3 == target).reshape(128, 128).astype(BF16)
        rows = pl.ds(pl.multiple_of(group * 128, 128), 128)
        oh[rows, :] = hot
        resp[pl.ds(group * 16, 16)] = dot(hot, patch).reshape(16, 8, 128).astype(BF16)

        deal(resp, fetched, 1, group, first)
        return carry

    serve(0, 0, first=1)
    lax.fori_loop(1, N_LAT, serve, 0)
    fetched[me] = resp[me]

    take_edges(mp, 0)
    loads[1].wait()
    sums = []
    for r in range(R):
        alpha = rec_s[0, r]

        def stencil(row, acc, r=r, alpha=alpha):
            damp = DAMP_WEIGHT * laplace_slab(mp, r, row) - alpha * dv[r, row]
            dp[r, row + 1, INNER] = damp
            return acc + fold(damp * damp)

        sums.append(lax.fori_loop(0, CLAT, stencil, jnp.zeros((8, 128), F32), unroll=2))
    send_edges(dp, 4)
    for j in range(8):
        blk = oh[j * 128 : (j + 1) * 128, :].astype(F32)
        oht[:, j * 128 : (j + 1) * 128] = blk.T.astype(BF16)
    ray_old = jnp.concatenate(
        [ray_v[:, b * RAYS_BLK : (b + 1) * RAYS_BLK] for b in range(RBMAX)]
        + [jnp.zeros((R, RAYS_BLK), F32)],
        axis=0,
    )
    wide16 = iota((16, RAYS_BLK), 0)
    r16 = wide16 & 3
    alpha16 = jnp.where(
        r16 == 0, rec_s[0, 0], jnp.where(r16 == 1, rec_s[0, 1], jnp.where(r16 == 2, rec_s[0, 2], rec_s[0, 3]))
    )
    ray_scaled = alpha16 * ray_old
    live = ((wide16 // 4) * RAYS_BLK + iota((16, RAYS_BLK), 1)) < cnt_s[0, 0]
    loads[2].wait()

    settle(fetched, recv_sem.at[1])
    blocks = fetched[...].reshape(1024, 128)
    for j in range(4):
        rows = slice(j * 256, (j + 1) * 256)
        wts[rows, :] = dot(sel[rows, :], blocks).astype(BF16)

    def forward(t, acc):
        rows = pl.ds(pl.multiple_of(t * 16, 16), 16)
        return acc + lax.dot_general(
            wts[rows, :], sens[t], (((1,), (1,)), ((), ())), preferred_element_type=F32
        )

    traced = lax.fori_loop(0, TILES, forward, jnp.zeros((16, RAYS_BLK), F32), unroll=6)
    ray_bar = jnp.where(live, traced - ray_scaled, 0.0)
    ray_keep[...] = ray_bar
    ray_sq = ray_bar * ray_bar
    ray_sq = ray_sq[:, 0:128] + ray_sq[:, 128:256]
    message = jnp.zeros((1, 128), F32)
    for r in range(R):
        part = jnp.where((row16 & 3) == r, ray_sq, 0.0)
        part = part[0:8] + part[8:16] + sums[r]
        message = jnp.where(iota((1, 128), 1) == r, jnp.sum(part, keepdims=True), message)
    sum_a[...] = message
    gather_lon(sum_a, part_a, 2)

    ray_low = ray_bar.astype(BF16)

    def adjoint(t, carry):
        term = dot(ray_low, sens[t])
        high = term.astype(BF16)
        rows = pl.ds(pl.multiple_of(t * 16, 16), 16)
        terms[rows, 0:128] = high
        terms[rows, 128:256] = (term - high.astype(F32)).astype(BF16)
        return carry

    lax.fori_loop(0, TILES, adjoint, 0, unroll=6)
    gather_lat(row_a, part_a, sums_a, 2)

    def give(c, carry, first=0):
        group = turn(c)
        rows = pl.ds(pl.multiple_of(group * 128, 128), 128)
        both = dot(selt[rows, :], terms[...])
        outg[pl.ds(group * 16, 16)] = (both[:, 0:128] + both[:, 128:256]).reshape(16, 8, 128)

        deal(outg, inc, 3, group, first)
        return carry

    give(0, 0, first=1)
    lax.fori_loop(1, N_LAT, give, 0)
    inc[me] = outg[me]

    take_edges(dp, 4)
    for r in range(R):

        def stencil2(row, carry, r=r):
            dv[r, row] = DAMP_WEIGHT * laplace_slab(dp, r, row)
            return carry

        lax.fori_loop(0, CLAT, stencil2, 0, unroll=2)

    settle(sums_a, recv_sem.at[6], N_LAT - 1)
    lane_sum = jnp.sum(sums_a[...], axis=0)[:, 0:R]
    beta = jnp.sqrt(lane_sum / ROWS_ALL + EPSILON)
    inv_beta = 1.0 / beta
    rho_bar = rec_v[1:2, :]
    phi_bar = rec_v[2:3, :]
    rho = jnp.sqrt(rho_bar * rho_bar + beta * beta)
    cosine = rho_bar / rho
    sine = beta / rho

    settle(inc, recv_sem.at[3])
    arrived = inc[...].reshape(1024, 128)
    high = arrived.astype(BF16)
    low = (arrived - high.astype(F32)).astype(BF16)
    image = dot(oht[...], high) + dot(oht[...], low)
    for r in range(R):
        for i in range(4):
            zbuf[r, i, pl.ds(32, 8), :] = image[r * 32 + i * 8 : r * 32 + i * 8 + 8]

    message = jnp.zeros((1, 128), F32)
    for r in range(R):
        beta_r = beta[:, r : r + 1]
        inv_r = inv_beta[:, r : r + 1]

        def renew(row, acc, r=r, beta_r=beta_r, inv_r=inv_r):
            off = row - lat0
            pick = jnp.where((off >= 0) & (off < 4), off, 4)
            extra = zbuf[r, pick, pl.ds(32 - lon0, CLON), :]
            upd = (dv[r, row] + extra) * inv_r - beta_r * mp[r, row + 1, INNER]
            upd_o[r, row] = upd
            return acc + fold(upd * upd)

        acc = lax.fori_loop(0, CLAT, renew, jnp.zeros((8, 128), F32), unroll=2)
        message = jnp.where(iota((1, 128), 1) == r, jnp.sum(acc, keepdims=True), message)
    sum_b[...] = message
    gather_lon(sum_b, part_b, 4)

    loads[3].wait()
    loads[4].wait()
    for r in range(R):
        for b in range(RBMAX):
            ray_o[r : r + 1, b * RAYS_BLK : (b + 1) * RAYS_BLK] = (
                ray_keep[4 * b + r : 4 * b + r + 1, :] * inv_beta[:, r : r + 1]
            )
    gain = cosine * phi_bar / rho
    for r in range(R):
        inv_r = inv_beta[:, r : r + 1]
        gain_r = gain[:, r : r + 1]

        def scale(row, carry, r=r, inv_r=inv_r, gain_r=gain_r):
            damp_o[r, row] = dp[r, row + 1, INNER] * inv_r
            sol_o[r, row] = sol_o[r, row] + gain_r * search_o[r, row]
            return carry

        lax.fori_loop(0, CLAT, scale, 0, unroll=2)
        if r == 1:
            gather_lat(row_b, part_b, sums_b, 4)

    settle(sums_b, recv_sem.at[8], N_LAT - 1)
    alpha_new = jnp.sqrt(jnp.sum(sums_b[...], axis=0)[:, 0:R] / CELLS + EPSILON)
    inv_alpha = 1.0 / alpha_new
    back = sine * alpha_new / rho
    for r in range(R):
        coef_o[r : r + 1, :] = jnp.broadcast_to(inv_alpha[:, r : r + 1], (1, 128))
        coef_o[4 + r : 5 + r, :] = jnp.broadcast_to(back[:, r : r + 1], (1, 128))
    rec_o[0:1, :] = alpha_new
    rec_o[1:2, :] = -cosine * alpha_new
    rec_o[2:3, :] = sine * phi_bar
    settle(ids_all, send_sem.at[0], N_LON - 1)
    settle(ids_all, send_sem.at[5], NDEV - N_LON)
    settle(fetched, send_sem.at[1])
    settle(part_a, send_sem.at[2], N_LON - 1)
    settle(sums_a, send_sem.at[6], N_LAT - 1)
    settle(inc, send_sem.at[3])
    settle(part_b, send_sem.at[4], N_LON - 1)
    settle(sums_b, send_sem.at[8], N_LAT - 1)


def finish_kernel(
    upd, damp, sol, search, coef, ray, rec,
    ray_out, damp_out, model_out, sol_out, search_out, rec_out,
    model_s, search_s, sem,
):
    copies = [
        pltpu.make_async_copy(damp, damp_out, sem.at[0]),
        pltpu.make_async_copy(sol, sol_out, sem.at[1]),
        pltpu.make_async_copy(ray, ray_out, sem.at[2]),
        pltpu.make_async_copy(rec, rec_out, sem.at[3]),
    ]
    for copy in copies:
        copy.start()
    for r in range(R):
        inv_r = coef[r : r + 1, :]
        back_r = coef[4 + r : 5 + r, :]

        def write(row, carry, r=r, inv_r=inv_r, back_r=back_r):
            model = upd[r, row] * inv_r
            model_s[r, row] = model
            search_s[r, row] = model - back_r * search[r, row]
            return carry

        lax.fori_loop(0, CLAT, write, 0, unroll=4)
        for src, dst, k in ((model_s, model_out, 4), (search_s, search_out, 8)):
            copy = pltpu.make_async_copy(src.at[r], dst.at[r], sem.at[k + r])
            copy.start()
            copies.append(copy)
    for copy in copies:
        copy.wait()


def per_device(
    sensitivity, block_ids, block_offsets, ray_counts, ray_vector, damping_vector, model_vector,
    solution, search, recurrence,
):
    field = (R, CLAT, CLON, DEPTH)
    vmem = pl.BlockSpec(memory_space=pltpu.VMEM)
    smem = pl.BlockSpec(memory_space=pltpu.SMEM)
    hbm = pl.BlockSpec(memory_space=pl.ANY)
    ids = block_ids.reshape(1, TILES)
    padded = (R, LAT_PAD, LON_PAD, DEPTH)
    middle = [
        pltpu.VMEM(field, F32), pltpu.VMEM(field, F32), pltpu.VMEM(field, F32), pltpu.VMEM(field, F32),
        pltpu.VMEM((8, 128), F32), pltpu.VMEM((R, RBMAX * RAYS_BLK), F32), pltpu.VMEM((3, R), F32),
    ]
    kept = pl.pallas_call(
        step_kernel,
        out_shape=middle,
        in_specs=[smem, smem, smem, smem, vmem, vmem, vmem, hbm, hbm, hbm, hbm, hbm],
        out_specs=[vmem] * 7,
        scratch_shapes=[
            pltpu.VMEM(padded, F32),
            pltpu.VMEM(padded, F32),
            pltpu.VMEM(field, F32),
            pltpu.VMEM((TILES, RAYS_BLK, DEPTH), BF16),
            pltpu.VMEM((1, 128), jnp.int32),
            pltpu.VMEM((NDEV, 1, 128), jnp.int32),
            pltpu.VMEM((64, 128), jnp.int32),
            pltpu.VMEM((64, 128), jnp.int32),
            pltpu.VMEM((1024, 128), F32),
            pltpu.VMEM((1024, 1024), BF16),
            pltpu.VMEM((1024, 1024), BF16),
            pltpu.VMEM((1024, 128), BF16),
            pltpu.VMEM((128, 1024), BF16),
            pltpu.VMEM((NDEV, 8, 128), BF16),
            pltpu.VMEM((NDEV, 8, 128), BF16),
            pltpu.VMEM((1024, 128), BF16),
            pltpu.VMEM((1024, 256), BF16),
            pltpu.VMEM((NDEV, 8, 128), F32),
            pltpu.VMEM((NDEV, 8, 128), F32),
            pltpu.VMEM((R, 5, 72, DEPTH), F32),
            pltpu.VMEM((1, 128), F32),
            pltpu.VMEM((N_LON, 1, 128), F32),
            pltpu.VMEM((1, 128), F32),
            pltpu.VMEM((N_LAT, 1, 128), F32),
            pltpu.VMEM((1, 128), F32),
            pltpu.VMEM((N_LON, 1, 128), F32),
            pltpu.VMEM((1, 128), F32),
            pltpu.VMEM((N_LAT, 1, 128), F32),
            pltpu.VMEM((2, 2, R, CLAT, DEPTH), F32),
            pltpu.VMEM((2, 2, R, CLAT, DEPTH), F32),
            pltpu.VMEM((2, 2, R, CLON, DEPTH), F32),
            pltpu.VMEM((16, RAYS_BLK), F32),
            pltpu.SemaphoreType.DMA((5,)),
            pltpu.SemaphoreType.DMA((9,)),
            pltpu.SemaphoreType.DMA((9,)),
            pltpu.SemaphoreType.DMA((8,)),
            pltpu.SemaphoreType.DMA((8,)),
        ],
        compiler_params=pltpu.CompilerParams(
            collective_id=0, has_side_effects=True, vmem_limit_bytes=48 * 1024 * 1024
        ),
        name="step",
    )(
        ids, block_offsets.reshape(1, RBMAX + 1), ray_counts, recurrence, ids, recurrence,
        ray_vector.reshape(R, RBMAX * RAYS_BLK), sensitivity.reshape(TILES, RAYS_BLK, DEPTH),
        damping_vector, model_vector, solution, search,
    )
    shapes = [(R, RBMAX * RAYS_BLK), field, field, field, field, (3, R)]
    ray_out, damp_out, model_out, sol_out, search_out, rec_out = pl.pallas_call(
        finish_kernel,
        out_shape=[jax.ShapeDtypeStruct(s, F32) for s in shapes],
        in_specs=[vmem] * 7,
        out_specs=[hbm] * 6,
        scratch_shapes=[
            pltpu.VMEM(field, F32), pltpu.VMEM(field, F32), pltpu.SemaphoreType.DMA((12,)),
        ],
        compiler_params=pltpu.CompilerParams(vmem_limit_bytes=24 * 1024 * 1024),
        name="finish",
    )(*kept)
    ray_out = ray_out.reshape(R, 1, 1, RBMAX * RAYS_BLK)
    return (ray_out, damp_out, model_out, sol_out, search_out, rec_out)


def solution(mesh):
    wide = P(None, "lat", "lon", None)
    return jax.shard_map(
        per_device,
        mesh=mesh,
        in_specs=(
            P("lat", "lon", None, None, None),
            P("lat", "lon", None),
            P("lat", "lon", None),
            P("lat", "lon"),
            wide,
            wide,
            wide,
            wide,
            wide,
            P(),
        ),
        out_specs=(wide, wide, wide, wide, wide, P()),
        check_vma=False,
    )
```

```python
import jax
import jax.numpy as jnp
from jax import lax
from jax.experimental import pallas as pl
from jax.experimental.pallas import tpu as pltpu
from jax.sharding import PartitionSpec as P

DAMP_WEIGHT = 0.15
EPSILON = 1e-05
MESH = pl.DeviceIdType.MESH
F32 = jnp.float32
BF16 = jnp.bfloat16

R = 4
CLAT = 32
CLON = 32
DEPTH = 128
BLK = CLAT * CLON
TILES = 60
RAYS_BLK = 256
RBMAX = 3
N_LAT = 8
N_LON = 16
NDEV = N_LAT * N_LON
LAT_PAD = CLAT + 2
LON_PAD = CLON + 16
LEFT = 8
ROWS_ALL = NDEV * RBMAX * RAYS_BLK + NDEV * BLK * DEPTH
CELLS = NDEV * BLK * DEPTH
INNER = pl.ds(LEFT, CLON)


def iota(shape, axis):
    return lax.broadcasted_iota(jnp.int32, shape, axis)


def one(cond):
    return jnp.where(cond, 1.0, 0.0)


def dot(a, b):
    return jnp.dot(a, b, preferred_element_type=F32)


def laplace_slab(ref, r, row):
    here = ref[r, row + 1, INNER]
    beside = ref[r, row, INNER] + ref[r, row + 2, INNER]
    beside = beside + ref[r, row + 1, pl.ds(LEFT - 1, CLON)] + ref[r, row + 1, pl.ds(LEFT + 1, CLON)]
    lane = iota((CLON, DEPTH), 1)
    above = jnp.where(lane == 0, 0.0, pltpu.roll(here, 1, 1))
    below = jnp.where(lane == DEPTH - 1, 0.0, pltpu.roll(here, DEPTH - 1, 1))
    return 6.0 * here - (beside + above + below)


def fold(x):
    return x[0:8] + x[8:16] + x[16:24] + x[24:32]


def step_kernel(
    ids_s, off_s, cnt_s, rec_s, ids_v, rec_v, ray_v, sens_h, damp_h, model_h, sol_h, search_h,
    upd_o, damp_o, sol_o, search_o, coef_o, ray_o, rec_o,
    mp, dp, dv, sens, idrow, ids_all, idcol, slotcol, rowval, sel, selt, oh, oht,
    resp, fetched, wts, terms, outg, inc, zbuf, sum_a, part_a, row_a, sums_a, sum_b, part_b, row_b, sums_b,
    edge_s, edge_r, row_r, ray_keep,
    load_sem, send_sem, recv_sem, edge_ssem, edge_rsem,
):
    my_lat = lax.axis_index("lat")
    my_lon = lax.axis_index("lon")
    me = my_lat * N_LON + my_lon

    barrier = pltpu.get_barrier_semaphore()

    def along_lon(step):
        return (my_lat, lax.rem(my_lon + step, N_LON))

    def along_lat(step):
        return (lax.rem(my_lat + step, N_LAT), my_lon)

    def greet_lon(step, carry):
        pl.semaphore_signal(barrier, inc=1, device_id=along_lon(step), device_id_type=MESH)
        return carry

    def greet_lat(step, carry):
        pl.semaphore_signal(barrier, inc=1, device_id=along_lat(step), device_id_type=MESH)
        return carry

    lax.fori_loop(1, N_LON, greet_lon, 0, unroll=True)
    lax.fori_loop(1, N_LAT, greet_lat, 0, unroll=True)

    loads = [
        pltpu.make_async_copy(model_h, mp.at[:, pl.ds(1, CLAT), INNER, :], load_sem.at[0]),
        pltpu.make_async_copy(damp_h, dv, load_sem.at[1]),
        pltpu.make_async_copy(sens_h, sens, load_sem.at[2]),
        pltpu.make_async_copy(sol_h, sol_o, load_sem.at[3]),
        pltpu.make_async_copy(search_h, search_o, load_sem.at[4]),
    ]
    loads[0].start()
    loads[1].start()

    idrow[...] = jnp.full((1, 128), -1, jnp.int32)
    idrow[:, 0:TILES] = ids_v[...]

    side = jnp.zeros((R, LAT_PAD, LEFT, DEPTH), F32)
    mp[:, :, pl.ds(0, LEFT), :] = side
    mp[:, :, pl.ds(LEFT + CLON, LEFT), :] = side
    dp[:, :, pl.ds(0, LEFT), :] = side
    dp[:, :, pl.ds(LEFT + CLON, LEFT), :] = side
    flat = jnp.zeros((R, CLON, DEPTH), F32)

    @pl.when(my_lat == 0)
    def _():
        mp[:, 0, INNER, :] = flat
        dp[:, 0, INNER, :] = flat

    @pl.when(my_lat == N_LAT - 1)
    def _():
        mp[:, LAT_PAD - 1, INNER, :] = flat
        dp[:, LAT_PAD - 1, INNER, :] = flat

    for t in range(TILES):
        idcol[t : t + 1, :] = jnp.full((1, 128), ids_s[0, t], jnp.int32)
    idcol[TILES:64, :] = jnp.full((64 - TILES, 128), -1, jnp.int32)
    owner_col = idcol[...] >> 10
    owner_row = jnp.broadcast_to(idrow[...] >> 10, (64, 128))
    twin = one((owner_col == owner_row) & (iota((64, 128), 1) < iota((64, 128), 0)))
    rank = jnp.max(twin, axis=1, keepdims=True).astype(jnp.int32)
    slotcol[...] = jnp.where(iota((64, 128), 0) < TILES, (owner_col * 2 + rank) * 4, -64)

    row16 = iota((16, 128), 0)
    blk16 = row16 // 4
    first16 = jnp.where(blk16 == 0, off_s[0, 0], jnp.where(blk16 == 1, off_s[0, 1], off_s[0, 2]))
    last16 = jnp.where(
        blk16 == 0, off_s[0, 1],
        jnp.where(blk16 == 1, off_s[0, 2], jnp.where(blk16 == 2, off_s[0, 3], 0)),
    )
    lane16 = iota((16, 128), 1)

    def build_sel(t, carry):
        slot = jnp.broadcast_to(slotcol[pl.ds(t, 1), :], (16, 128))
        value = jnp.where((first16 <= t) & (t < last16), slot + (row16 & 3), -1)
        rows = pl.ds(pl.multiple_of(t * 16, 16), 16)
        rowval[rows, :] = value.astype(F32)
        for j in range(8):
            sel[rows, j * 128 : (j + 1) * 128] = one(value == lane16 + j * 128).astype(BF16)
        return carry

    lax.fori_loop(0, 64, build_sel, 0, unroll=2)

    pl.semaphore_wait(barrier, N_LON - 1 + N_LAT - 1)

    def spread(src, dst, k, count, along):
        def send(step, carry):
            pltpu.make_async_remote_copy(
                src, dst, send_sem.at[k], recv_sem.at[k],
                device_id=along(step), device_id_type=MESH,
            ).start()
            return carry

        lax.fori_loop(1, count, send, 0, unroll=True)

    def settle(dst, sem, rows=NDEV - 1):
        most = dst.at[pl.ds(0, rows)]
        pltpu.make_async_copy(most, most, sem).wait()

    spread(idrow, ids_all.at[me], 0, N_LON, along_lon)
    ids_all[me] = idrow[...]

    def edge(buf, k, base):
        n = base + k
        if k == 0:
            src, dst, to = buf.at[:, 1, INNER, :], row_r.at[base // 4, 1], (my_lat - 1, my_lon)
        elif k == 1:
            src, dst, to = buf.at[:, CLAT, INNER, :], row_r.at[base // 4, 0], (my_lat + 1, my_lon)
        elif k == 2:
            src, dst, to = edge_s.at[base // 4, 0], edge_r.at[base // 4, 1], (my_lat, my_lon - 1)
        else:
            src, dst, to = edge_s.at[base // 4, 1], edge_r.at[base // 4, 0], (my_lat, my_lon + 1)
        return pltpu.make_async_remote_copy(
            src, dst, edge_ssem.at[n], edge_rsem.at[n], device_id=to, device_id_type=MESH
        )

    has = [my_lat > 0, my_lat < N_LAT - 1, my_lon > 0, my_lon < N_LON - 1]
    opposite = [1, 0, 3, 2]

    def send_edges(buf, base):
        for r in range(R):
            edge_s[base // 4, 0, r] = buf[r, pl.ds(1, CLAT), LEFT, :]
            edge_s[base // 4, 1, r] = buf[r, pl.ds(1, CLAT), LEFT + CLON - 1, :]
        for k in range(4):
            @pl.when(has[k])
            def _(k=k):
                edge(buf, k, base).start()

    def take_edges(buf, base):
        for k in range(4):
            @pl.when(has[k])
            def _(k=k):
                edge(buf, opposite[k], base).wait_recv()
                edge(buf, k, base).wait_send()
        for k, row in ((0, 0), (1, LAT_PAD - 1)):
            @pl.when(has[k])
            def _(k=k, row=row):
                for r in range(R):
                    buf[r, row, INNER, :] = row_r[base // 4, k, r]
        for k, column in ((2, LEFT - 1), (3, LEFT + CLON)):
            @pl.when(has[k])
            def _(k=k, column=column):
                for r in range(R):
                    buf[r, pl.ds(1, CLAT), column, :] = edge_r[base // 4, k - 2, r]

    def build_selt(g, carry):
        rows = pl.ds(pl.multiple_of(g * 16, 16), 16)
        number = (row16 + g * 16).astype(F32)
        for j in range(8):
            lanes = jnp.broadcast_to(rowcol[j], (16, 128))
            selt[rows, j * 128 : (j + 1) * 128] = one(lanes == number).astype(BF16)
        return carry

    rowcol = [rowval[j * 128 : (j + 1) * 128, :].T[0:1, :] for j in range(8)]
    lax.fori_loop(0, 64, build_selt, 0, unroll=2)
    row_ids = ids_all.at[pl.ds(my_lat * N_LON, N_LON)]
    settle(ids_all, recv_sem.at[0], N_LON - 1)
    spread(row_ids, row_ids, 5, N_LAT, along_lat)
    loads[0].wait()
    loads[2].start()
    send_edges(mp, 0)
    zbuf[...] = jnp.zeros_like(zbuf)
    terms[TILES * 16 : 1024, :] = jnp.zeros((1024 - TILES * 16, 256), BF16)

    def gather_lon(src, parts, k):
        spread(src, parts.at[my_lon], k, N_LON, along_lon)
        parts[my_lon] = src[...]

    def gather_lat(row_sum, parts, totals, k):
        settle(parts, recv_sem.at[k], N_LON - 1)
        row_sum[...] = jnp.sum(parts[...], axis=0)
        spread(row_sum, totals.at[my_lat], k + 4, N_LAT, along_lat)
        totals[my_lat] = row_sum[...]

    settle(ids_all, recv_sem.at[5], NDEV - N_LON)
    asked = ids_all[...]
    mine = (asked >> 10) == me
    lat0 = jnp.min(jnp.where(mine, (asked >> 5) & 31, CLAT - 4))
    lon0 = jnp.min(jnp.where(mine, asked & 31, CLON - 4))
    patch = jnp.concatenate(
        [mp[r, lat0 + i + 1, pl.ds(LEFT + lon0, 8), :] for r in range(R) for i in range(4)], axis=0
    ).astype(BF16)

    sub3 = iota((16, 8, 128), 1)
    lane3 = iota((16, 8, 128), 2)
    sign3 = jnp.where(sub3 < 4, 1.0, -1.0)

    def turn(c):
        return lax.rem(my_lat + c, N_LAT)

    def deal(src, dst, k, group, first):
        def send(s, carry):
            lon = lax.rem(my_lon + 5 * s, N_LON)
            pltpu.make_async_remote_copy(
                src.at[group * N_LON + lon], dst.at[me], send_sem.at[k], recv_sem.at[k],
                device_id=(group, lon), device_id_type=MESH,
            ).start()
            return carry

        lax.fori_loop(first, N_LON, send, 0, unroll=True)

    def serve(c, carry, first=0):
        group = turn(c)
        near = jnp.broadcast_to(ids_all[pl.ds(group * 16, 16)], (16, 8, 128))
        cell = (((near >> 5) & 31) - lat0) * 8 + ((near & 31) - lon0)
        key = (lane3 * 64 + cell).astype(F32) * sign3
        least = jnp.min(jnp.where((near >> 10) == me, key, 1e6), axis=2, keepdims=True)
        pick = jnp.abs(least).astype(jnp.int32)
        target = jnp.where(pick < 64 * 128, (sub3 & 3) * 32 + (pick & 63), -1)
        hot = one(lane3 == target).reshape(128, 128).astype(BF16)
        rows = pl.ds(pl.multiple_of(group * 128, 128), 128)
        oh[rows, :] = hot
        resp[pl.ds(group * 16, 16)] = dot(hot, patch).reshape(16, 8, 128).astype(BF16)

        deal(resp, fetched, 1, group, first)
        return carry

    serve(0, 0, first=1)
    lax.fori_loop(1, N_LAT, serve, 0)
    fetched[me] = resp[me]
    loads[3].start()
    loads[4].start()

    take_edges(mp, 0)
    loads[1].wait()
    sums = []
    for r in range(R):
        alpha = rec_s[0, r]

        def stencil(row, acc, r=r, alpha=alpha):
            damp = DAMP_WEIGHT * laplace_slab(mp, r, row) - alpha * dv[r, row]
            dp[r, row + 1, INNER] = damp
            return acc + fold(damp * damp)

        sums.append(lax.fori_loop(0, CLAT, stencil, jnp.zeros((8, 128), F32), unroll=2))
    send_edges(dp, 4)
    for j in range(8):
        blk = oh[j * 128 : (j + 1) * 128, :].astype(F32)
        oht[:, j * 128 : (j + 1) * 128] = blk.T.astype(BF16)
    ray_old = jnp.concatenate(
        [ray_v[r, 0, :, b * RAYS_BLK : (b + 1) * RAYS_BLK] for b in range(RBMAX) for r in range(R)]
        + [jnp.zeros((R, RAYS_BLK), F32)],
        axis=0,
    )
    wide16 = iota((16, RAYS_BLK), 0)
    r16 = wide16 & 3
    alpha16 = jnp.where(
        r16 == 0, rec_s[0, 0], jnp.where(r16 == 1, rec_s[0, 1], jnp.where(r16 == 2, rec_s[0, 2], rec_s[0, 3]))
    )
    ray_scaled = alpha16 * ray_old
    live = ((wide16 // 4) * RAYS_BLK + iota((16, RAYS_BLK), 1)) < cnt_s[0, 0]
    loads[2].wait()

    settle(fetched, recv_sem.at[1])
    blocks = fetched[...].reshape(1024, 128)
    for j in range(4):
        rows = slice(j * 256, (j + 1) * 256)
        wts[rows, :] = dot(sel[rows, :], blocks).astype(BF16)

    def forward(t, acc):
        rows = pl.ds(pl.multiple_of(t * 16, 16), 16)
        return acc + lax.dot_general(
            wts[rows, :], sens[t], (((1,), (1,)), ((), ())), preferred_element_type=F32
        )

    traced = lax.fori_loop(0, TILES, forward, jnp.zeros((16, RAYS_BLK), F32), unroll=6)
    ray_bar = jnp.where(live, traced - ray_scaled, 0.0)
    ray_keep[...] = ray_bar
    ray_sq = ray_bar * ray_bar
    ray_sq = ray_sq[:, 0:128] + ray_sq[:, 128:256]
    message = jnp.zeros((1, 128), F32)
    for r in range(R):
        part = jnp.where((row16 & 3) == r, ray_sq, 0.0)
        part = part[0:8] + part[8:16] + sums[r]
        message = jnp.where(iota((1, 128), 1) == r, jnp.sum(part, keepdims=True), message)
    sum_a[...] = message
    gather_lon(sum_a, part_a, 2)

    ray_low = ray_bar.astype(BF16)

    def adjoint(t, carry):
        term = dot(ray_low, sens[t])
        high = term.astype(BF16)
        rows = pl.ds(pl.multiple_of(t * 16, 16), 16)
        terms[rows, 0:128] = high
        terms[rows, 128:256] = (term - high.astype(F32)).astype(BF16)
        return carry

    lax.fori_loop(0, TILES, adjoint, 0, unroll=6)

    def give(c, carry, first=0):
        group = turn(c)
        rows = pl.ds(pl.multiple_of(group * 128, 128), 128)
        both = dot(selt[rows, :], terms[...])
        outg[pl.ds(group * 16, 16)] = (both[:, 0:128] + both[:, 128:256]).reshape(16, 8, 128)

        deal(outg, inc, 3, group, first)
        return carry

    give(0, 0, first=1)
    lax.fori_loop(1, N_LAT, give, 0)
    inc[me] = outg[me]
    gather_lat(row_a, part_a, sums_a, 2)

    take_edges(dp, 4)
    for r in range(R):

        def stencil2(row, carry, r=r):
            dv[r, row] = DAMP_WEIGHT * laplace_slab(dp, r, row)
            return carry

        lax.fori_loop(0, CLAT, stencil2, 0, unroll=2)

    settle(sums_a, recv_sem.at[6], N_LAT - 1)
    lane_sum = jnp.sum(sums_a[...], axis=0)[:, 0:R]
    beta = jnp.sqrt(lane_sum / ROWS_ALL + EPSILON)
    inv_beta = 1.0 / beta
    rho_bar = rec_v[1:2, :]
    phi_bar = rec_v[2:3, :]
    rho = jnp.sqrt(rho_bar * rho_bar + beta * beta)
    cosine = rho_bar / rho
    sine = beta / rho

    settle(inc, recv_sem.at[3])
    arrived = inc[...].reshape(1024, 128)
    high = arrived.astype(BF16)
    low = (arrived - high.astype(F32)).astype(BF16)
    image = dot(oht[...], high) + dot(oht[...], low)
    for r in range(R):
        for i in range(4):
            zbuf[r, i, pl.ds(32, 8), :] = image[r * 32 + i * 8 : r * 32 + i * 8 + 8]

    message = jnp.zeros((1, 128), F32)
    for r in range(R):
        beta_r = beta[:, r : r + 1]
        inv_r = inv_beta[:, r : r + 1]

        def renew(row, acc, r=r, beta_r=beta_r, inv_r=inv_r):
            off = row - lat0
            pick = jnp.where((off >= 0) & (off < 4), off, 4)
            extra = zbuf[r, pick, pl.ds(32 - lon0, CLON), :]
            upd = (dv[r, row] + extra) * inv_r - beta_r * mp[r, row + 1, INNER]
            upd_o[r, row] = upd
            return acc + fold(upd * upd)

        acc = lax.fori_loop(0, CLAT, renew, jnp.zeros((8, 128), F32), unroll=2)
        message = jnp.where(iota((1, 128), 1) == r, jnp.sum(acc, keepdims=True), message)
    sum_b[...] = message
    gather_lon(sum_b, part_b, 4)

    loads[3].wait()
    loads[4].wait()
    for r in range(R):
        for b in range(RBMAX):
            ray_o[r, 0, :, b * RAYS_BLK : (b + 1) * RAYS_BLK] = (
                ray_keep[4 * b + r : 4 * b + r + 1, :] * inv_beta[:, r : r + 1]
            )
    gain = cosine * phi_bar / rho
    for r in range(R):
        inv_r = inv_beta[:, r : r + 1]
        gain_r = gain[:, r : r + 1]

        def scale(row, carry, r=r, inv_r=inv_r, gain_r=gain_r):
            damp_o[r, row] = dp[r, row + 1, INNER] * inv_r
            sol_o[r, row] = sol_o[r, row] + gain_r * search_o[r, row]
            return carry

        lax.fori_loop(0, CLAT, scale, 0, unroll=2)
        if r == 1:
            gather_lat(row_b, part_b, sums_b, 4)

    settle(sums_b, recv_sem.at[8], N_LAT - 1)
    alpha_new = jnp.sqrt(jnp.sum(sums_b[...], axis=0)[:, 0:R] / CELLS + EPSILON)
    inv_alpha = 1.0 / alpha_new
    back = sine * alpha_new / rho
    for r in range(R):
        coef_o[r : r + 1, :] = jnp.broadcast_to(inv_alpha[:, r : r + 1], (1, 128))
        coef_o[4 + r : 5 + r, :] = jnp.broadcast_to(back[:, r : r + 1], (1, 128))
    rec_o[0:1, :] = alpha_new
    rec_o[1:2, :] = -cosine * alpha_new
    rec_o[2:3, :] = sine * phi_bar
    settle(ids_all, send_sem.at[0], N_LON - 1)
    settle(ids_all, send_sem.at[5], NDEV - N_LON)
    settle(fetched, send_sem.at[1])
    settle(part_a, send_sem.at[2], N_LON - 1)
    settle(sums_a, send_sem.at[6], N_LAT - 1)
    settle(inc, send_sem.at[3])
    settle(part_b, send_sem.at[4], N_LON - 1)
    settle(sums_b, send_sem.at[8], N_LAT - 1)


def finish_kernel(
    upd, damp, sol, search, coef, ray, rec,
    ray_out, damp_out, model_out, sol_out, search_out, rec_out,
    model_s, search_s, sem,
):
    copies = [
        pltpu.make_async_copy(damp, damp_out, sem.at[0]),
        pltpu.make_async_copy(sol, sol_out, sem.at[1]),
        pltpu.make_async_copy(ray, ray_out, sem.at[2]),
        pltpu.make_async_copy(rec, rec_out, sem.at[3]),
    ]
    for copy in copies:
        copy.start()
    for r in range(R):
        inv_r = coef[r : r + 1, :]
        back_r = coef[4 + r : 5 + r, :]

        def write(row, carry, r=r, inv_r=inv_r, back_r=back_r):
            model = upd[r, row] * inv_r
            model_s[r, row] = model
            search_s[r, row] = model - back_r * search[r, row]
            return carry

        lax.fori_loop(0, CLAT, write, 0, unroll=4)
        for src, dst, k in ((model_s, model_out, 4), (search_s, search_out, 8)):
            copy = pltpu.make_async_copy(src.at[r], dst.at[r], sem.at[k + r])
            copy.start()
            copies.append(copy)
    for copy in copies:
        copy.wait()


def per_device(
    sensitivity, block_ids, block_offsets, ray_counts, ray_vector, damping_vector, model_vector,
    solution, search, recurrence,
):
    field = (R, CLAT, CLON, DEPTH)
    vmem = pl.BlockSpec(memory_space=pltpu.VMEM)
    smem = pl.BlockSpec(memory_space=pltpu.SMEM)
    hbm = pl.BlockSpec(memory_space=pl.ANY)
    ids = block_ids.reshape(1, TILES)
    padded = (R, LAT_PAD, LON_PAD, DEPTH)
    middle = [
        pltpu.VMEM(field, F32), pltpu.VMEM(field, F32), pltpu.VMEM(field, F32), pltpu.VMEM(field, F32),
        pltpu.VMEM((8, 128), F32), pltpu.VMEM((R, 1, 1, RBMAX * RAYS_BLK), F32), pltpu.VMEM((3, R), F32),
    ]
    kept = pl.pallas_call(
        step_kernel,
        out_shape=middle,
        in_specs=[smem, smem, smem, smem, vmem, vmem, vmem, hbm, hbm, hbm, hbm, hbm],
        out_specs=[vmem] * 7,
        scratch_shapes=[
            pltpu.VMEM(padded, F32),
            pltpu.VMEM(padded, F32),
            pltpu.VMEM(field, F32),
            pltpu.VMEM((TILES, RAYS_BLK, DEPTH), BF16),
            pltpu.VMEM((1, 128), jnp.int32),
            pltpu.VMEM((NDEV, 1, 128), jnp.int32),
            pltpu.VMEM((64, 128), jnp.int32),
            pltpu.VMEM((64, 128), jnp.int32),
            pltpu.VMEM((1024, 128), F32),
            pltpu.VMEM((1024, 1024), BF16),
            pltpu.VMEM((1024, 1024), BF16),
            pltpu.VMEM((1024, 128), BF16),
            pltpu.VMEM((128, 1024), BF16),
            pltpu.VMEM((NDEV, 8, 128), BF16),
            pltpu.VMEM((NDEV, 8, 128), BF16),
            pltpu.VMEM((1024, 128), BF16),
            pltpu.VMEM((1024, 256), BF16),
            pltpu.VMEM((NDEV, 8, 128), F32),
            pltpu.VMEM((NDEV, 8, 128), F32),
            pltpu.VMEM((R, 5, 72, DEPTH), F32),
            pltpu.VMEM((1, 128), F32),
            pltpu.VMEM((N_LON, 1, 128), F32),
            pltpu.VMEM((1, 128), F32),
            pltpu.VMEM((N_LAT, 1, 128), F32),
            pltpu.VMEM((1, 128), F32),
            pltpu.VMEM((N_LON, 1, 128), F32),
            pltpu.VMEM((1, 128), F32),
            pltpu.VMEM((N_LAT, 1, 128), F32),
            pltpu.VMEM((2, 2, R, CLAT, DEPTH), F32),
            pltpu.VMEM((2, 2, R, CLAT, DEPTH), F32),
            pltpu.VMEM((2, 2, R, CLON, DEPTH), F32),
            pltpu.VMEM((16, RAYS_BLK), F32),
            pltpu.SemaphoreType.DMA((5,)),
            pltpu.SemaphoreType.DMA((9,)),
            pltpu.SemaphoreType.DMA((9,)),
            pltpu.SemaphoreType.DMA((8,)),
            pltpu.SemaphoreType.DMA((8,)),
        ],
        compiler_params=pltpu.CompilerParams(
            collective_id=0, has_side_effects=True, vmem_limit_bytes=48 * 1024 * 1024
        ),
        name="step",
    )(
        ids, block_offsets.reshape(1, RBMAX + 1), ray_counts, recurrence, ids, recurrence,
        ray_vector, sensitivity.reshape(TILES, RAYS_BLK, DEPTH),
        damping_vector, model_vector, solution, search,
    )
    shapes = [(R, 1, 1, RBMAX * RAYS_BLK), field, field, field, field, (3, R)]
    ray_out, damp_out, model_out, sol_out, search_out, rec_out = pl.pallas_call(
        finish_kernel,
        out_shape=[jax.ShapeDtypeStruct(s, F32) for s in shapes],
        in_specs=[vmem] * 7,
        out_specs=[hbm] * 6,
        scratch_shapes=[
            pltpu.VMEM(field, F32), pltpu.VMEM(field, F32), pltpu.SemaphoreType.DMA((12,)),
        ],
        compiler_params=pltpu.CompilerParams(vmem_limit_bytes=24 * 1024 * 1024),
        name="finish",
    )(*kept)
    return (ray_out, damp_out, model_out, sol_out, search_out, rec_out)


def solution(mesh):
    wide = P(None, "lat", "lon", None)
    return jax.shard_map(
        per_device,
        mesh=mesh,
        in_specs=(
            P("lat", "lon", None, None, None),
            P("lat", "lon", None),
            P("lat", "lon", None),
            P("lat", "lon"),
            wide,
            wide,
            wide,
            wide,
            wide,
            P(),
        ),
        out_specs=(wide, wide, wide, wide, wide, P()),
        check_vma=False,
    )
```

```python
import jax
import jax.numpy as jnp
from jax import lax
from jax.experimental import pallas as pl
from jax.experimental.pallas import tpu as pltpu
from jax.sharding import PartitionSpec as P

DAMP_WEIGHT = 0.15
EPSILON = 1e-05
MESH = pl.DeviceIdType.MESH
F32 = jnp.float32
BF16 = jnp.bfloat16

R = 4
CLAT = 32
CLON = 32
DEPTH = 128
BLK = CLAT * CLON
TILES = 60
RAYS_BLK = 256
RBMAX = 3
N_LAT = 8
N_LON = 16
NDEV = N_LAT * N_LON
LAT_PAD = CLAT + 2
LON_PAD = CLON + 16
LEFT = 8
ROWS_ALL = NDEV * RBMAX * RAYS_BLK + NDEV * BLK * DEPTH
CELLS = NDEV * BLK * DEPTH
INNER = pl.ds(LEFT, CLON)


def iota(shape, axis):
    return lax.broadcasted_iota(jnp.int32, shape, axis)


def one(cond):
    return jnp.where(cond, 1.0, 0.0)


def dot(a, b):
    return jnp.dot(a, b, preferred_element_type=F32)


def laplace_slab(ref, r, row):
    here = ref[r, row + 1, INNER]
    beside = ref[r, row, INNER] + ref[r, row + 2, INNER]
    beside = beside + ref[r, row + 1, pl.ds(LEFT - 1, CLON)] + ref[r, row + 1, pl.ds(LEFT + 1, CLON)]
    lane = iota((CLON, DEPTH), 1)
    above = jnp.where(lane == 0, 0.0, pltpu.roll(here, 1, 1))
    below = jnp.where(lane == DEPTH - 1, 0.0, pltpu.roll(here, DEPTH - 1, 1))
    return 6.0 * here - (beside + above + below)


def fold(x):
    return x[0:8] + x[8:16] + x[16:24] + x[24:32]


def step_kernel(
    ids_s, off_s, cnt_s, rec_s, ids_v, rec_v, ray_v, sens_h, damp_h, model_h, sol_h, search_h,
    upd_o, damp_o, sol_o, search_o, coef_o, ray_o, rec_o,
    mp, dp, dv, sens, idrow, ids_all, idcol, slotcol, rowval, sel, selt, oh, oht,
    resp, fetched, wts, terms, outg, inc, zbuf, sum_a, part_a, row_a, sums_a, sum_b, part_b, row_b, sums_b,
    edge_s, edge_r, row_r, ray_keep,
    load_sem, send_sem, recv_sem, edge_ssem, edge_rsem,
):
    my_lat = lax.axis_index("lat")
    my_lon = lax.axis_index("lon")
    me = my_lat * N_LON + my_lon

    barrier = pltpu.get_barrier_semaphore()

    def along_lon(step):
        return (my_lat, lax.rem(my_lon + step, N_LON))

    def along_lat(step):
        return (lax.rem(my_lat + step, N_LAT), my_lon)

    def greet_lon(step, carry):
        pl.semaphore_signal(barrier, inc=1, device_id=along_lon(step), device_id_type=MESH)
        return carry

    def greet_lat(step, carry):
        pl.semaphore_signal(barrier, inc=1, device_id=along_lat(step), device_id_type=MESH)
        return carry

    lax.fori_loop(1, N_LON, greet_lon, 0, unroll=True)
    lax.fori_loop(1, N_LAT, greet_lat, 0, unroll=True)

    loads = [
        pltpu.make_async_copy(model_h, mp.at[:, pl.ds(1, CLAT), INNER, :], load_sem.at[0]),
        pltpu.make_async_copy(damp_h, dv, load_sem.at[1]),
        pltpu.make_async_copy(sens_h, sens, load_sem.at[2]),
        pltpu.make_async_copy(sol_h, sol_o, load_sem.at[3]),
        pltpu.make_async_copy(search_h, search_o, load_sem.at[4]),
    ]
    loads[0].start()
    loads[1].start()

    idrow[...] = jnp.full((1, 128), -1, jnp.int32)
    idrow[:, 0:TILES] = ids_v[...]

    side = jnp.zeros((R, LAT_PAD, LEFT, DEPTH), F32)
    mp[:, :, pl.ds(0, LEFT), :] = side
    mp[:, :, pl.ds(LEFT + CLON, LEFT), :] = side
    dp[:, :, pl.ds(0, LEFT), :] = side
    dp[:, :, pl.ds(LEFT + CLON, LEFT), :] = side
    flat = jnp.zeros((R, CLON, DEPTH), F32)

    @pl.when(my_lat == 0)
    def _():
        mp[:, 0, INNER, :] = flat
        dp[:, 0, INNER, :] = flat

    @pl.when(my_lat == N_LAT - 1)
    def _():
        mp[:, LAT_PAD - 1, INNER, :] = flat
        dp[:, LAT_PAD - 1, INNER, :] = flat

    for t in range(TILES):
        idcol[t : t + 1, :] = jnp.full((1, 128), ids_s[0, t], jnp.int32)
    idcol[TILES:64, :] = jnp.full((64 - TILES, 128), -1, jnp.int32)
    owner_col = idcol[...] >> 10
    owner_row = jnp.broadcast_to(idrow[...] >> 10, (64, 128))
    twin = one((owner_col == owner_row) & (iota((64, 128), 1) < iota((64, 128), 0)))
    rank = jnp.max(twin, axis=1, keepdims=True).astype(jnp.int32)
    slotcol[...] = jnp.where(iota((64, 128), 0) < TILES, (owner_col * 2 + rank) * 4, -64)

    row16 = iota((16, 128), 0)
    blk16 = row16 // 4
    first16 = jnp.where(blk16 == 0, off_s[0, 0], jnp.where(blk16 == 1, off_s[0, 1], off_s[0, 2]))
    last16 = jnp.where(
        blk16 == 0, off_s[0, 1],
        jnp.where(blk16 == 1, off_s[0, 2], jnp.where(blk16 == 2, off_s[0, 3], 0)),
    )
    lane16 = iota((16, 128), 1)

    def build_sel(t, carry):
        slot = jnp.broadcast_to(slotcol[pl.ds(t, 1), :], (16, 128))
        value = jnp.where((first16 <= t) & (t < last16), slot + (row16 & 3), -1)
        rows = pl.ds(pl.multiple_of(t * 16, 16), 16)
        rowval[rows, :] = value.astype(F32)
        for j in range(8):
            sel[rows, j * 128 : (j + 1) * 128] = one(value == lane16 + j * 128).astype(BF16)
        return carry

    lax.fori_loop(0, 64, build_sel, 0, unroll=2)

    pl.semaphore_wait(barrier, N_LON - 1 + N_LAT - 1)

    def spread(src, dst, k, count, along):
        def send(step, carry):
            pltpu.make_async_remote_copy(
                src, dst, send_sem.at[k], recv_sem.at[k],
                device_id=along(step), device_id_type=MESH,
            ).start()
            return carry

        lax.fori_loop(1, count, send, 0, unroll=True)

    def settle(dst, sem, rows=NDEV - 1):
        most = dst.at[pl.ds(0, rows)]
        pltpu.make_async_copy(most, most, sem).wait()

    spread(idrow, ids_all.at[me], 0, N_LON, along_lon)
    ids_all[me] = idrow[...]

    def edge(buf, k, base):
        n = base + k
        if k == 0:
            src, dst, to = buf.at[:, 1, INNER, :], row_r.at[base // 4, 1], (my_lat - 1, my_lon)
        elif k == 1:
            src, dst, to = buf.at[:, CLAT, INNER, :], row_r.at[base // 4, 0], (my_lat + 1, my_lon)
        elif k == 2:
            src, dst, to = edge_s.at[base // 4, 0], edge_r.at[base // 4, 1], (my_lat, my_lon - 1)
        else:
            src, dst, to = edge_s.at[base // 4, 1], edge_r.at[base // 4, 0], (my_lat, my_lon + 1)
        return pltpu.make_async_remote_copy(
            src, dst, edge_ssem.at[n], edge_rsem.at[n], device_id=to, device_id_type=MESH
        )

    has = [my_lat > 0, my_lat < N_LAT - 1, my_lon > 0, my_lon < N_LON - 1]
    opposite = [1, 0, 3, 2]

    def send_edges(buf, base):
        for r in range(R):
            edge_s[base // 4, 0, r] = buf[r, pl.ds(1, CLAT), LEFT, :]
            edge_s[base // 4, 1, r] = buf[r, pl.ds(1, CLAT), LEFT + CLON - 1, :]
        for k in range(4):
            @pl.when(has[k])
            def _(k=k):
                edge(buf, k, base).start()

    def take_edges(buf, base):
        for k in range(4):
            @pl.when(has[k])
            def _(k=k):
                edge(buf, opposite[k], base).wait_recv()
                edge(buf, k, base).wait_send()
        for k, row in ((0, 0), (1, LAT_PAD - 1)):
            @pl.when(has[k])
            def _(k=k, row=row):
                for r in range(R):
                    buf[r, row, INNER, :] = row_r[base // 4, k, r]
        for k, column in ((2, LEFT - 1), (3, LEFT + CLON)):
            @pl.when(has[k])
            def _(k=k, column=column):
                for r in range(R):
                    buf[r, pl.ds(1, CLAT), column, :] = edge_r[base // 4, k - 2, r]

    def build_selt(g, carry):
        rows = pl.ds(pl.multiple_of(g * 16, 16), 16)
        number = (row16 + g * 16).astype(F32)
        for j in range(8):
            lanes = jnp.broadcast_to(rowcol[j], (16, 128))
            selt[rows, j * 128 : (j + 1) * 128] = one(lanes == number).astype(BF16)
        return carry

    rowcol = [rowval[j * 128 : (j + 1) * 128, :].T[0:1, :] for j in range(8)]
    lax.fori_loop(0, 64, build_selt, 0, unroll=2)
    row_ids = ids_all.at[pl.ds(my_lat * N_LON, N_LON)]
    settle(ids_all, recv_sem.at[0], N_LON - 1)
    spread(row_ids, row_ids, 5, N_LAT, along_lat)
    loads[0].wait()
    loads[2].start()
    send_edges(mp, 0)
    zbuf[...] = jnp.zeros_like(zbuf)
    terms[TILES * 16 : 1024, :] = jnp.zeros((1024 - TILES * 16, 256), BF16)

    def gather_lon(src, parts, k):
        spread(src, parts.at[my_lon], k, N_LON, along_lon)
        parts[my_lon] = src[...]

    def gather_lat(row_sum, parts, totals, k):
        settle(parts, recv_sem.at[k], N_LON - 1)
        row_sum[...] = jnp.sum(parts[...], axis=0)
        spread(row_sum, totals.at[my_lat], k + 4, N_LAT, along_lat)
        totals[my_lat] = row_sum[...]

    settle(ids_all, recv_sem.at[5], NDEV - N_LON)
    asked = ids_all[...]
    mine = (asked >> 10) == me
    lat0 = jnp.min(jnp.where(mine, (asked >> 5) & 31, CLAT - 4))
    lon0 = jnp.min(jnp.where(mine, asked & 31, CLON - 4))
    patch = jnp.concatenate(
        [mp[r, lat0 + i + 1, pl.ds(LEFT + lon0, 8), :] for r in range(R) for i in range(4)], axis=0
    ).astype(BF16)

    sub3 = iota((16, 8, 128), 1)
    lane3 = iota((16, 8, 128), 2)
    sign3 = jnp.where(sub3 < 4, 1.0, -1.0)

    def turn(c):
        return lax.rem(my_lat + 1 + lax.rem(c + 3, N_LAT - 1), N_LAT)

    def deal(src, dst, k, group, first):
        def send(s, carry):
            lon = lax.rem(my_lon + 5 * s, N_LON)
            pltpu.make_async_remote_copy(
                src.at[group * N_LON + lon], dst.at[me], send_sem.at[k], recv_sem.at[k],
                device_id=(group, lon), device_id_type=MESH,
            ).start()
            return carry

        lax.fori_loop(first, N_LON, send, 0, unroll=True)

    def serve(c, carry, first=0):
        group = my_lat if first else turn(c)
        near = jnp.broadcast_to(ids_all[pl.ds(group * 16, 16)], (16, 8, 128))
        cell = (((near >> 5) & 31) - lat0) * 8 + ((near & 31) - lon0)
        key = (lane3 * 64 + cell).astype(F32) * sign3
        least = jnp.min(jnp.where((near >> 10) == me, key, 1e6), axis=2, keepdims=True)
        pick = jnp.abs(least).astype(jnp.int32)
        target = jnp.where(pick < 64 * 128, (sub3 & 3) * 32 + (pick & 63), -1)
        hot = one(lane3 == target).reshape(128, 128).astype(BF16)
        rows = pl.ds(pl.multiple_of(group * 128, 128), 128)
        oh[rows, :] = hot
        resp[pl.ds(group * 16, 16)] = dot(hot, patch).reshape(16, 8, 128).astype(BF16)

        deal(resp, fetched, 1, group, first)
        return carry

    lax.fori_loop(0, N_LAT - 1, serve, 0)
    serve(None, 0, first=1)
    fetched[me] = resp[me]
    loads[3].start()
    loads[4].start()

    take_edges(mp, 0)
    loads[1].wait()
    sums = []
    for r in range(R):
        alpha = rec_s[0, r]

        def stencil(row, acc, r=r, alpha=alpha):
            damp = DAMP_WEIGHT * laplace_slab(mp, r, row) - alpha * dv[r, row]
            dp[r, row + 1, INNER] = damp
            return acc + fold(damp * damp)

        sums.append(lax.fori_loop(0, CLAT, stencil, jnp.zeros((8, 128), F32), unroll=2))
    send_edges(dp, 4)
    for j in range(8):
        blk = oh[j * 128 : (j + 1) * 128, :].astype(F32)
        oht[:, j * 128 : (j + 1) * 128] = blk.T.astype(BF16)
    ray_old = jnp.concatenate(
        [ray_v[r, 0, :, b * RAYS_BLK : (b + 1) * RAYS_BLK] for b in range(RBMAX) for r in range(R)]
        + [jnp.zeros((R, RAYS_BLK), F32)],
        axis=0,
    )
    wide16 = iota((16, RAYS_BLK), 0)
    r16 = wide16 & 3
    alpha16 = jnp.where(
        r16 == 0, rec_s[0, 0], jnp.where(r16 == 1, rec_s[0, 1], jnp.where(r16 == 2, rec_s[0, 2], rec_s[0, 3]))
    )
    ray_scaled = alpha16 * ray_old
    live = ((wide16 // 4) * RAYS_BLK + iota((16, RAYS_BLK), 1)) < cnt_s[0, 0]
    loads[2].wait()

    settle(fetched, recv_sem.at[1])
    blocks = fetched[...].reshape(1024, 128)
    for j in range(4):
        rows = slice(j * 256, (j + 1) * 256)
        wts[rows, :] = dot(sel[rows, :], blocks).astype(BF16)

    def forward(t, acc):
        rows = pl.ds(pl.multiple_of(t * 16, 16), 16)
        return acc + lax.dot_general(
            wts[rows, :], sens[t], (((1,), (1,)), ((), ())), preferred_element_type=F32
        )

    traced = lax.fori_loop(0, TILES, forward, jnp.zeros((16, RAYS_BLK), F32), unroll=6)
    ray_bar = jnp.where(live, traced - ray_scaled, 0.0)
    ray_keep[...] = ray_bar
    ray_sq = ray_bar * ray_bar
    ray_sq = ray_sq[:, 0:128] + ray_sq[:, 128:256]
    message = jnp.zeros((1, 128), F32)
    for r in range(R):
        part = jnp.where((row16 & 3) == r, ray_sq, 0.0)
        part = part[0:8] + part[8:16] + sums[r]
        message = jnp.where(iota((1, 128), 1) == r, jnp.sum(part, keepdims=True), message)
    sum_a[...] = message
    gather_lon(sum_a, part_a, 2)

    ray_low = ray_bar.astype(BF16)

    def adjoint(t, carry):
        term = dot(ray_low, sens[t])
        high = term.astype(BF16)
        rows = pl.ds(pl.multiple_of(t * 16, 16), 16)
        terms[rows, 0:128] = high
        terms[rows, 128:256] = (term - high.astype(F32)).astype(BF16)
        return carry

    lax.fori_loop(0, TILES, adjoint, 0, unroll=6)

    def give(c, carry, first=0):
        group = my_lat if first else turn(c)
        rows = pl.ds(pl.multiple_of(group * 128, 128), 128)
        both = dot(selt[rows, :], terms[...])
        outg[pl.ds(group * 16, 16)] = (both[:, 0:128] + both[:, 128:256]).reshape(16, 8, 128)

        deal(outg, inc, 3, group, first)
        return carry

    lax.fori_loop(0, N_LAT - 1, give, 0)
    give(None, 0, first=1)
    inc[me] = outg[me]
    gather_lat(row_a, part_a, sums_a, 2)

    take_edges(dp, 4)
    for r in range(R):

        def stencil2(row, carry, r=r):
            dv[r, row] = DAMP_WEIGHT * laplace_slab(dp, r, row)
            return carry

        lax.fori_loop(0, CLAT, stencil2, 0, unroll=2)

    settle(sums_a, recv_sem.at[6], N_LAT - 1)
    lane_sum = jnp.sum(sums_a[...], axis=0)[:, 0:R]
    beta = jnp.sqrt(lane_sum / ROWS_ALL + EPSILON)
    inv_beta = 1.0 / beta
    rho_bar = rec_v[1:2, :]
    phi_bar = rec_v[2:3, :]
    rho = jnp.sqrt(rho_bar * rho_bar + beta * beta)
    cosine = rho_bar / rho
    sine = beta / rho

    settle(inc, recv_sem.at[3])
    arrived = inc[...].reshape(1024, 128)
    high = arrived.astype(BF16)
    low = (arrived - high.astype(F32)).astype(BF16)
    image = dot(oht[...], high) + dot(oht[...], low)
    for r in range(R):
        for i in range(4):
            zbuf[r, i, pl.ds(32, 8), :] = image[r * 32 + i * 8 : r * 32 + i * 8 + 8]

    message = jnp.zeros((1, 128), F32)
    for r in range(R):
        beta_r = beta[:, r : r + 1]
        inv_r = inv_beta[:, r : r + 1]

        def renew(row, acc, r=r, beta_r=beta_r, inv_r=inv_r):
            off = row - lat0
            pick = jnp.where((off >= 0) & (off < 4), off, 4)
            extra = zbuf[r, pick, pl.ds(32 - lon0, CLON), :]
            upd = (dv[r, row] + extra) * inv_r - beta_r * mp[r, row + 1, INNER]
            upd_o[r, row] = upd
            return acc + fold(upd * upd)

        acc = lax.fori_loop(0, CLAT, renew, jnp.zeros((8, 128), F32), unroll=2)
        message = jnp.where(iota((1, 128), 1) == r, jnp.sum(acc, keepdims=True), message)
    sum_b[...] = message
    gather_lon(sum_b, part_b, 4)

    loads[3].wait()
    loads[4].wait()
    for r in range(R):
        for b in range(RBMAX):
            ray_o[r, 0, :, b * RAYS_BLK : (b + 1) * RAYS_BLK] = (
                ray_keep[4 * b + r : 4 * b + r + 1, :] * inv_beta[:, r : r + 1]
            )
    gain = cosine * phi_bar / rho
    for r in range(R):
        inv_r = inv_beta[:, r : r + 1]
        gain_r = gain[:, r : r + 1]

        def scale(row, carry, r=r, inv_r=inv_r, gain_r=gain_r):
            damp_o[r, row] = dp[r, row + 1, INNER] * inv_r
            sol_o[r, row] = sol_o[r, row] + gain_r * search_o[r, row]
            return carry

        lax.fori_loop(0, CLAT, scale, 0, unroll=2)
        if r == 1:
            gather_lat(row_b, part_b, sums_b, 4)

    settle(sums_b, recv_sem.at[8], N_LAT - 1)
    alpha_new = jnp.sqrt(jnp.sum(sums_b[...], axis=0)[:, 0:R] / CELLS + EPSILON)
    inv_alpha = 1.0 / alpha_new
    back = sine * alpha_new / rho
    for r in range(R):
        coef_o[r : r + 1, :] = jnp.broadcast_to(inv_alpha[:, r : r + 1], (1, 128))
        coef_o[4 + r : 5 + r, :] = jnp.broadcast_to(back[:, r : r + 1], (1, 128))
    rec_o[0:1, :] = alpha_new
    rec_o[1:2, :] = -cosine * alpha_new
    rec_o[2:3, :] = sine * phi_bar
    settle(ids_all, send_sem.at[0], N_LON - 1)
    settle(ids_all, send_sem.at[5], NDEV - N_LON)
    settle(fetched, send_sem.at[1])
    settle(part_a, send_sem.at[2], N_LON - 1)
    settle(sums_a, send_sem.at[6], N_LAT - 1)
    settle(inc, send_sem.at[3])
    settle(part_b, send_sem.at[4], N_LON - 1)
    settle(sums_b, send_sem.at[8], N_LAT - 1)


def finish_kernel(
    upd, damp, sol, search, coef, ray, rec,
    ray_out, damp_out, model_out, sol_out, search_out, rec_out,
    model_s, search_s, sem,
):
    copies = [
        pltpu.make_async_copy(damp, damp_out, sem.at[0]),
        pltpu.make_async_copy(sol, sol_out, sem.at[1]),
        pltpu.make_async_copy(ray, ray_out, sem.at[2]),
        pltpu.make_async_copy(rec, rec_out, sem.at[3]),
    ]
    for copy in copies:
        copy.start()
    for r in range(R):
        inv_r = coef[r : r + 1, :]
        back_r = coef[4 + r : 5 + r, :]

        def write(row, carry, r=r, inv_r=inv_r, back_r=back_r):
            model = upd[r, row] * inv_r
            model_s[r, row] = model
            search_s[r, row] = model - back_r * search[r, row]
            return carry

        lax.fori_loop(0, CLAT, write, 0, unroll=4)
        for src, dst, k in ((model_s, model_out, 4), (search_s, search_out, 8)):
            copy = pltpu.make_async_copy(src.at[r], dst.at[r], sem.at[k + r])
            copy.start()
            copies.append(copy)
    for copy in copies:
        copy.wait()


def per_device(
    sensitivity, block_ids, block_offsets, ray_counts, ray_vector, damping_vector, model_vector,
    solution, search, recurrence,
):
    field = (R, CLAT, CLON, DEPTH)
    vmem = pl.BlockSpec(memory_space=pltpu.VMEM)
    smem = pl.BlockSpec(memory_space=pltpu.SMEM)
    hbm = pl.BlockSpec(memory_space=pl.ANY)
    ids = block_ids.reshape(1, TILES)
    padded = (R, LAT_PAD, LON_PAD, DEPTH)
    middle = [
        pltpu.VMEM(field, F32), pltpu.VMEM(field, F32), pltpu.VMEM(field, F32), pltpu.VMEM(field, F32),
        pltpu.VMEM((8, 128), F32), pltpu.VMEM((R, 1, 1, RBMAX * RAYS_BLK), F32), pltpu.VMEM((3, R), F32),
    ]
    kept = pl.pallas_call(
        step_kernel,
        out_shape=middle,
        in_specs=[smem, smem, smem, smem, vmem, vmem, vmem, hbm, hbm, hbm, hbm, hbm],
        out_specs=[vmem] * 7,
        scratch_shapes=[
            pltpu.VMEM(padded, F32),
            pltpu.VMEM(padded, F32),
            pltpu.VMEM(field, F32),
            pltpu.VMEM((TILES, RAYS_BLK, DEPTH), BF16),
            pltpu.VMEM((1, 128), jnp.int32),
            pltpu.VMEM((NDEV, 1, 128), jnp.int32),
            pltpu.VMEM((64, 128), jnp.int32),
            pltpu.VMEM((64, 128), jnp.int32),
            pltpu.VMEM((1024, 128), F32),
            pltpu.VMEM((1024, 1024), BF16),
            pltpu.VMEM((1024, 1024), BF16),
            pltpu.VMEM((1024, 128), BF16),
            pltpu.VMEM((128, 1024), BF16),
            pltpu.VMEM((NDEV, 8, 128), BF16),
            pltpu.VMEM((NDEV, 8, 128), BF16),
            pltpu.VMEM((1024, 128), BF16),
            pltpu.VMEM((1024, 256), BF16),
            pltpu.VMEM((NDEV, 8, 128), F32),
            pltpu.VMEM((NDEV, 8, 128), F32),
            pltpu.VMEM((R, 5, 72, DEPTH), F32),
            pltpu.VMEM((1, 128), F32),
            pltpu.VMEM((N_LON, 1, 128), F32),
            pltpu.VMEM((1, 128), F32),
            pltpu.VMEM((N_LAT, 1, 128), F32),
            pltpu.VMEM((1, 128), F32),
            pltpu.VMEM((N_LON, 1, 128), F32),
            pltpu.VMEM((1, 128), F32),
            pltpu.VMEM((N_LAT, 1, 128), F32),
            pltpu.VMEM((2, 2, R, CLAT, DEPTH), F32),
            pltpu.VMEM((2, 2, R, CLAT, DEPTH), F32),
            pltpu.VMEM((2, 2, R, CLON, DEPTH), F32),
            pltpu.VMEM((16, RAYS_BLK), F32),
            pltpu.SemaphoreType.DMA((5,)),
            pltpu.SemaphoreType.DMA((9,)),
            pltpu.SemaphoreType.DMA((9,)),
            pltpu.SemaphoreType.DMA((8,)),
            pltpu.SemaphoreType.DMA((8,)),
        ],
        compiler_params=pltpu.CompilerParams(
            collective_id=0, has_side_effects=True, vmem_limit_bytes=48 * 1024 * 1024
        ),
        name="step",
    )(
        ids, block_offsets.reshape(1, RBMAX + 1), ray_counts, recurrence, ids, recurrence,
        ray_vector, sensitivity.reshape(TILES, RAYS_BLK, DEPTH),
        damping_vector, model_vector, solution, search,
    )
    shapes = [(R, 1, 1, RBMAX * RAYS_BLK), field, field, field, field, (3, R)]
    ray_out, damp_out, model_out, sol_out, search_out, rec_out = pl.pallas_call(
        finish_kernel,
        out_shape=[jax.ShapeDtypeStruct(s, F32) for s in shapes],
        in_specs=[vmem] * 7,
        out_specs=[hbm] * 6,
        scratch_shapes=[
            pltpu.VMEM(field, F32), pltpu.VMEM(field, F32), pltpu.SemaphoreType.DMA((12,)),
        ],
        compiler_params=pltpu.CompilerParams(vmem_limit_bytes=24 * 1024 * 1024),
        name="finish",
    )(*kept)
    return (ray_out, damp_out, model_out, sol_out, search_out, rec_out)


def solution(mesh):
    wide = P(None, "lat", "lon", None)
    return jax.shard_map(
        per_device,
        mesh=mesh,
        in_specs=(
            P("lat", "lon", None, None, None),
            P("lat", "lon", None),
            P("lat", "lon", None),
            P("lat", "lon"),
            wide,
            wide,
            wide,
            wide,
            wide,
            P(),
        ),
        out_specs=(wide, wide, wide, wide, wide, P()),
        check_vma=False,
    )
```
